256 devices in a mesh: param: 64 (over x, z, y_hi), sensor: 4 (over y_lo, core).
Axes of the slice: x: 4, y: 4 (y_hi: 2, y_lo: 2; y = y_hi * 2 + y_lo), z: 8, core: 2. Of those that a mesh axis runs over, the one named last changes fastest.
Arguments:
- readings: bfloat16 [64, 600, 128], P('param', 'sensor'), may hold values from -6 to 6
- spectra: bfloat16 [2, 65, 600, 8192], P(None, None, 'sensor', 'param'), may hold values from -0.0625 to 0.0625
- stiffness: float32 [8192], P('param'), may hold values from 0.04 to 0.24
Outputs:
- hessian_panel: float32 [64, 600, 128], P('param', 'sensor')
The draws below stay inside these ranges and needn't reach their ends.
All inputs are finite; a program needn't handle non-finite values.
Results may differ from the reference program's by a relative error of at most 0.0025.
Values may be sent and summed in bfloat16 or wider, within the bound.
No kernel may reach another device: no remote copies, remote signals or barrier semaphores. Data moves between devices by JAX's collectives and lax.ppermute only.
A program may use at most 128 MiB of HBM per device.

```python
import math
import jax
import jax.numpy as jnp
from jax import lax

SENSORS = 600
STEPS = 64
NB = 65
GY = 64
NCOL = 128
GX = 128
M = 8192


def block_levels(stream_key, extent, cuts, smallest, top_value):
    def one(dim, shards_of):
        heights = jax.random.uniform(jax.random.fold_in(jax.random.fold_in(stream_key, 6), dim), (shards_of,), jnp.float32, smallest / len(cuts), top_value / len(cuts))
        return jnp.repeat(jnp.exp(heights), extent[dim] // shards_of).reshape((-1,) + (1,) * (len(extent) - dim - 1))

    loudness = one(*cuts[0])
    for cut in cuts[1:]:
        loudness = loudness * one(*cut)
    return loudness


def scatter_about(own_key, extent, spread, limit, cuts=(), kind=jnp.bfloat16):
    result = spread * jax.random.normal(own_key, extent, jnp.float32)
    if cuts:
        result = result * block_levels(own_key, extent, cuts, -0.22, 0.18)
    return jnp.clip(result, -limit, limit).astype(kind)


def setup_inputs(seed: int = 0) -> dict:
    seeds = jax.random.split(jax.random.key(seed), 4)
    return {
        "readings": scatter_about(seeds[0], (STEPS, SENSORS, NCOL), 1.0, 6.0, ((0, 64), (1, 4))),
        "spectra": scatter_about(seeds[1], (2, NB, SENSORS, M), M ** -0.5, 0.0625, ((2, 4), (3, 64))),
        "stiffness": jnp.clip(jnp.exp(math.log(0.24) - 1.7917595 * jax.random.uniform(seeds[2], (M,), jnp.float32) ** block_levels(seeds[2], (M,), ((0, 64),), -0.2, 0.2)), 0.04, 0.24),
    }


def angles(bins, times):
    prod = bins[:, None] * times[None, :] % (2 * STEPS)
    return prod.astype(jnp.float32) * (2.0 * math.pi / (2 * STEPS))

def forward_tables():
    bins = jnp.arange(STEPS + 1, dtype=jnp.int32)
    times = jnp.arange(STEPS, dtype=jnp.int32)
    phase_angle = angles(bins, times)
    scale_factor = 1.0 / math.sqrt(STEPS)
    return (jnp.cos(phase_angle) * scale_factor, jnp.sin(phase_angle) * scale_factor)

def inverse_tables():
    bins = jnp.arange(STEPS + 1, dtype=jnp.int32)
    times = jnp.arange(STEPS, dtype=jnp.int32)
    phase_angle = angles(bins, times)
    weight = jnp.where((bins == 0) | (bins == STEPS), 1.0, 2.0).astype(jnp.float32)[:, None]
    scale_factor = 1.0 / math.sqrt(STEPS)
    return ((jnp.cos(phase_angle) * weight * scale_factor).T, (jnp.sin(phase_angle) * weight * scale_factor).T)

def transform(value_entries):
    cosine_table, sine_table = forward_tables()
    hessian_product = lax.Precision.HIGHEST
    real_part = jnp.einsum('uo,ojm->ujm', cosine_table, value_entries, precision=hessian_product)
    imaginary_part = -jnp.einsum('uo,ojm->ujm', sine_table, value_entries, precision=hessian_product)
    return (real_part, imaginary_part)

def untransform(real_part, imaginary_part):
    cosine_inverse, sine_inverse = inverse_tables()
    hessian_product = lax.Precision.HIGHEST
    return jnp.einsum('ni,ilj->nlj', cosine_inverse, real_part, precision=hessian_product) - jnp.einsum('ni,ilj->nlj', sine_inverse, imaginary_part, precision=hessian_product)

def reference(readings, spectra, stiffness):
    hessian_product = lax.Precision.HIGHEST
    data_re, data_im = transform(readings.astype(jnp.float32))
    data_re = data_re.astype(jnp.bfloat16)
    data_im = data_im.astype(jnp.bfloat16)

    def adjoint_bin(item_list):
        spectrum_real, spectrum_imaginary, dre, dim = [coeff_array.astype(jnp.float32) for coeff_array in item_list]
        real_part = jnp.dot(spectrum_real.T, dre, precision=hessian_product) + jnp.dot(spectrum_imaginary.T, dim, precision=hessian_product)
        imaginary_part = jnp.dot(spectrum_real.T, dim, precision=hessian_product) - jnp.dot(spectrum_imaginary.T, dre, precision=hessian_product)
        return (real_part, imaginary_part)
    adj_re, adj_im = lax.map(adjoint_bin, (spectra[0], spectra[1], data_re, data_im))
    field = untransform(adj_re, adj_im)
    grid = field.reshape(STEPS, GX, GY, NCOL)
    coeff = stiffness.reshape(GX, GY)[None, :, :, None]
    for sweep in range(2):
        padded = jnp.pad(grid, ((0, 0), (1, 1), (1, 1), (0, 0)))
        beside_all = padded[:, :-2, 1:-1] + padded[:, 2:, 1:-1] + padded[:, 1:-1, :-2] + padded[:, 1:-1, 2:]
        grid = grid + coeff * (beside_all - 4.0 * grid)
    smoothed = grid.reshape(STEPS, M, NCOL)
    model_re, model_im = transform(smoothed)
    model_re = model_re.astype(jnp.bfloat16)
    model_im = model_im.astype(jnp.bfloat16)

    def forward_bin(item_list):
        spectrum_real, spectrum_imaginary, vector_real, vector_imaginary = [coeff_array.astype(jnp.float32) for coeff_array in item_list]
        real_part = jnp.dot(spectrum_real, vector_real, precision=hessian_product) - jnp.dot(spectrum_imaginary, vector_imaginary, precision=hessian_product)
        imaginary_part = jnp.dot(spectrum_real, vector_imaginary, precision=hessian_product) + jnp.dot(spectrum_imaginary, vector_real, precision=hessian_product)
        return (real_part, imaginary_part)
    out_re, out_im = lax.map(forward_bin, (spectra[0], spectra[1], model_re, model_im))
    return untransform(out_re, out_im)
```

```python
import math

import jax
import jax.numpy as jnp
import numpy as np
from jax import lax
from jax.sharding import Mesh, PartitionSpec as P

STEPS = 64
NB = STEPS + 1
GY = 64
NCOL = 128
SPLIT = 80
BF = jnp.bfloat16
F32 = jnp.float32


def fetch(v, axis, count, d):
    return lax.ppermute(v, axis, [((i + d) % count, i) for i in range(count)])


def push(v, axis, count, d):
    return fetch(v, axis, count, -d)


def angle_tables():
    bins = np.arange(NB)[:, None]
    times = np.arange(STEPS)[None, :]
    angle = 2.0 * math.pi * ((bins * times) % (2 * STEPS)) / (2 * STEPS)
    scale = 1.0 / math.sqrt(STEPS)
    weight = np.where((bins == 0) | (bins == STEPS), 1.0, 2.0)
    forward = np.concatenate([np.cos(angle), -np.sin(angle)]) * scale
    inverse = np.concatenate([np.cos(angle) * weight, -np.sin(angle) * weight]) * scale
    return forward.astype(np.float32), inverse.astype(np.float32)


def two_parts(table):
    high = table.astype(BF)
    low = (table - high.astype(np.float32)).astype(BF)
    return high, low


def pick(table, steps):
    onehot = (jnp.arange(STEPS)[:, None] == steps[None, :]).astype(BF)
    return [
        jnp.dot(jnp.asarray(part), onehot, preferred_element_type=F32).astype(BF)
        for part in two_parts(table)
    ]


def transform(table, value):
    high, low = table
    eq = "ut,t...->u..."
    return jnp.einsum("ut,tjc->ujc", high, value, preferred_element_type=F32) + jnp.einsum(
        "ut,tjc->ujc", low, value, preferred_element_type=F32
    )


def untransform(table, real, imag):
    full = table[0].astype(F32) + table[1].astype(F32)
    return jnp.einsum(
        "un,ujc->njc", full[:NB], real, precision=lax.Precision.HIGHEST
    ) + jnp.einsum("un,ujc->njc", full[NB:], imag, precision=lax.Precision.HIGHEST)


Z_ORDER = (0, 1, 2, 3, 7, 6, 5, 4)
X_ORDER = (0, 1, 3, 2)


def gather_z(v):
    half = v.shape[0] // 2
    up = [v]
    down = [v]
    for _ in range(3):
        up.append(fetch(up[-1], "z", 8, 1))
        down.append(fetch(down[-1], "z", 8, -1))
    far_low = fetch(up[3][:half], "z", 8, 1)
    far_high = fetch(down[3][half:], "z", 8, -1)
    return jnp.concatenate(up + down[1:] + [far_low, far_high])


def gather_x(v):
    half = v.shape[0] // 2
    up = fetch(v, "x", 4, 1)
    down = fetch(v, "x", 4, -1)
    far_low = fetch(up[:half], "x", 4, 1)
    far_high = fetch(down[half:], "x", 4, -1)
    return jnp.concatenate([v, up, down, far_low, far_high])


def reduce_z(v):
    half = v.shape[1] // 2
    up = push(v[4, :half].astype(BF), "z", 8, 1)
    down = push(v[4, half:].astype(BF), "z", 8, -1)
    up = jnp.concatenate([v[3, :half] + up.astype(F32), v[3, half:]])
    down = jnp.concatenate([v[5, :half], v[5, half:] + down.astype(F32)])
    for d in (2, 1, 0):
        up = push(up.astype(BF), "z", 8, 1).astype(F32)
        down = push(down.astype(BF), "z", 8, -1).astype(F32)
        if d:
            up = v[d] + up
            down = v[8 - d] + down
    return v[0] + up + down


def reduce_x(v):
    half = v.shape[1] // 2
    up = push(v[2, :half].astype(BF), "x", 4, 1)
    down = push(v[2, half:].astype(BF), "x", 4, -1)
    up = jnp.concatenate([v[1, :half] + up.astype(F32), v[1, half:]])
    down = jnp.concatenate([v[3, :half], v[3, half:] + down.astype(F32)])
    up = push(up.astype(BF), "x", 4, 1).astype(F32)
    down = push(down.astype(BF), "x", 4, -1).astype(F32)
    return v[0] + up + down


def reduce_direct(v, axis, count):
    total = v[0]
    parts = [push(v[d].astype(BF), axis, count, d) for d in range(1, count)]
    for part in parts:
        total = total + part.astype(F32)
    return total


def swap(v, *axes):
    out = v
    names = tuple(axes)
    size = 2 ** len(names)
    return lax.ppermute(out, names, [(i, size - 1 - i) for i in range(size)])


def shards(readings, spectra, stiffness):
    x, z, yh = lax.axis_index("x"), lax.axis_index("z"), lax.axis_index("yh")
    yl, core = lax.axis_index("yl"), lax.axis_index("core")
    forward, inverse = angle_tables()

    def step_of(dx, dz, dy):
        return ((x + dx) % 4) * 16 + ((z + dz) % 8) * 2 + (yh ^ dy)

    zo, xo = jnp.array(Z_ORDER), jnp.array(X_ORDER)
    x4, z8, y2 = jnp.arange(4), jnp.arange(8), jnp.arange(2)
    steps_a = step_of(xo[None, :, None], zo[:, None, None], y2[None, None, :]).reshape(-1)
    steps_b = step_of(xo[:, None, None], zo[None, :, None], y2[None, None, :]).reshape(-1)
    steps_za = step_of(x4[None, :, None], z8[:, None, None], y2[None, None, :]).reshape(-1)
    steps_xb = step_of(x4[:, None, None], z8[None, :, None], y2[None, None, :]).reshape(-1)
    b8 = jnp.arange(2)
    place = (
        (core ^ b8[:, None, None]) * 4 + (yh ^ b8[None, :, None]) * 2 + (yl ^ b8[None, None, :])
    ).reshape(-1)
    steps_f = (place[:, None] * 8 + jnp.arange(8)[None, :]).reshape(-1)

    chain = [(i, i + 1) for i in range(31)]
    back = [(i + 1, i) for i in range(31)]
    other = swap(stiffness, "yh")
    coeff = jnp.where(
        yh == 0, jnp.concatenate([stiffness, other]), jnp.concatenate([other, stiffness])
    )
    coeff = jnp.concatenate(
        [
            lax.ppermute(coeff[-GY:], ("x", "z"), chain),
            coeff,
            lax.ppermute(coeff[:GY], ("x", "z"), back),
        ]
    ).reshape(6, GY)

    pair = jnp.concatenate([readings, swap(readings, "yh")])
    all_a = gather_z(gather_x(pair[:, :SPLIT]))
    all_b = gather_x(gather_z(pair[:, SPLIT:]))
    data = jnp.concatenate(
        [
            transform(pick(forward, steps_a), all_a).astype(BF),
            transform(pick(forward, steps_b), all_b).astype(BF),
        ],
        axis=1,
    )
    data_re, data_im = data[:NB], data[NB:]
    spectrum_real, spectrum_imaginary = spectra[0], spectra[1]
    adj_re = jnp.einsum(
        "ksm,ksc->kmc", spectrum_real, data_re, preferred_element_type=F32
    ) + jnp.einsum("ksm,ksc->kmc", spectrum_imaginary, data_im, preferred_element_type=F32)
    adj_im = jnp.einsum(
        "ksm,ksc->kmc", spectrum_real, data_im, preferred_element_type=F32
    ) - jnp.einsum("ksm,ksc->kmc", spectrum_imaginary, data_re, preferred_element_type=F32)
    field = untransform(pick(inverse, steps_f), adj_re, adj_im)

    points = field.shape[1]
    field = field[:32] + swap(field[32:].astype(BF), "core").astype(F32)
    field = field.reshape(2, 2, 8, points, NCOL)
    here = field[0, 0] + swap(field[0, 1].astype(BF), "yl").astype(F32)
    there = swap(field[1, 0].astype(BF), "yh").astype(F32) + swap(
        field[1, 1].astype(BF), "yh", "yl"
    ).astype(F32)
    here = here.reshape(8, 2, GY, NCOL)
    there = there.reshape(8, 2, GY, NCOL)
    grid = jnp.where(
        yh == 0, jnp.concatenate([here, there], axis=1), jnp.concatenate([there, here], axis=1)
    )
    low = lax.ppermute(grid[:, -2:].astype(BF), ("x", "z"), chain)
    high = lax.ppermute(grid[:, :2].astype(BF), ("x", "z"), back)
    grid = jnp.concatenate([low.astype(F32), grid, high.astype(F32)], axis=1)
    for sweep in range(2):
        inner = grid[:, 1:-1]
        sides = jnp.pad(inner, ((0, 0), (0, 0), (1, 1), (0, 0)))
        beside = grid[:, :-2] + grid[:, 2:] + sides[:, :, :-2] + sides[:, :, 2:]
        rows = coeff if sweep == 0 else coeff[1:-1]
        grid = inner + rows[None, :, :, None] * (beside - 4.0 * inner)
    grid = grid.astype(BF)
    here = jnp.where(yh == 0, grid[:, :2], grid[:, 2:])
    there = jnp.where(yh == 0, grid[:, 2:], grid[:, :2])
    half = jnp.concatenate(
        [here, swap(here, "yl"), swap(there, "yh"), swap(there, "yh", "yl")]
    ).reshape(32, points, NCOL)
    model = jnp.concatenate([half, swap(half, "core")])

    model = transform(pick(forward, steps_f), model).astype(BF)
    model_re, model_im = model[:NB], model[NB:]
    out_re = jnp.einsum(
        "ksm,kmc->ksc", spectrum_real, model_re, preferred_element_type=F32
    ) - jnp.einsum("ksm,kmc->ksc", spectrum_imaginary, model_im, preferred_element_type=F32)
    out_im = jnp.einsum(
        "ksm,kmc->ksc", spectrum_real, model_im, preferred_element_type=F32
    ) + jnp.einsum("ksm,kmc->ksc", spectrum_imaginary, model_re, preferred_element_type=F32)

    part_a = untransform(pick(inverse, steps_za), out_re[:, :SPLIT], out_im[:, :SPLIT])
    part_b = untransform(pick(inverse, steps_xb), out_re[:, SPLIT:], out_im[:, SPLIT:])
    part_a = reduce_z(part_a.reshape((8, 8) + part_a.shape[1:]))
    part_a = reduce_direct(part_a.reshape((4, 2) + part_a.shape[1:]), "x", 4)
    part_b = reduce_x(part_b.reshape((4, 16) + part_b.shape[1:]))
    part_b = reduce_direct(part_b.reshape((8, 2) + part_b.shape[1:]), "z", 8)
    both = jnp.concatenate([part_a, part_b], axis=1)
    return both[:1] + swap(both[1:], "yh")


def solution(mesh):
    fine = Mesh(mesh.devices.reshape(4, 8, 2, 2, 2), ("x", "z", "yh", "yl", "core"))
    param, sensor = ("x", "z", "yh"), ("yl", "core")
    return jax.shard_map(
        shards,
        mesh=fine,
        in_specs=(P(param, sensor, None), P(None, None, sensor, param), P(param)),
        out_specs=P(param, sensor, None),
        check_vma=False,
    )
```

```python
import math

import jax
import jax.numpy as jnp
import numpy as np
from jax import lax
from jax.experimental import pallas as pl
from jax.experimental.pallas import tpu as pltpu
from jax.sharding import Mesh, PartitionSpec as P

STEPS = 64
NB = STEPS + 1
GY = 64
NCOL = 128
BF = jnp.bfloat16
F32 = jnp.float32
ROWS = 152
FREQ = 136
PTS = 128


def forward_table(steps):
    bins = np.arange(NB)[:, None]
    angle = 2.0 * math.pi * (bins * np.asarray(steps)[None, :] % (2 * STEPS)) / (2 * STEPS)
    rows = np.concatenate([np.cos(angle), -np.sin(angle)]) / math.sqrt(STEPS)
    return np.pad(rows, ((0, FREQ - 2 * NB), (0, 0))).astype(np.float32)


def inverse_table(steps):
    weight = np.full(NB, 2.0, np.float32)
    weight[[0, STEPS]] = 1.0
    weight = np.pad(np.concatenate([weight, weight]), (0, FREQ - 2 * NB))
    return forward_table(steps).T * weight


def halves(value):
    high = value.astype(BF)
    return high, (value - high.astype(F32)).astype(BF)


def dot(a, b):
    return jnp.dot(a, b, preferred_element_type=F32)


def adjoint_kernel(
    read_ref, fwd_ref, inv_ref, spec_ref, keep_ref, give_ref, time_ref, data_ref, adj_ref, spec, sem
):
    copy = pltpu.make_async_copy(spec_ref, spec, sem)
    copy.start()
    for i in range(STEPS):
        time_ref[pl.ds(i * ROWS, ROWS), :] = read_ref[i].astype(F32)
    high, low = halves(fwd_ref[...])
    fwd = jnp.concatenate([high, low], axis=1)

    def to_bins(i, c):
        s0 = i * 4
        values = [time_ref[pl.ds(s0 + j, STEPS, stride=ROWS), :].astype(BF) for j in range(4)]
        block = jnp.concatenate(values, axis=1)
        result = dot(fwd, jnp.concatenate([block, block], axis=0))
        for j in range(4):
            data_ref[pl.ds(s0 + j, FREQ, stride=ROWS), :] = result[:, j * NCOL : (j + 1) * NCOL]
        return c

    lax.fori_loop(0, ROWS // 4, to_bins, 0)
    copy.wait()
    zero = jnp.zeros((PTS, NCOL), F32)
    for j in range(2 * NB, FREQ):
        adj_ref[pl.ds(j, PTS, stride=FREQ), :] = zero
    sensors = spec.shape[2]

    def one_bin(k):
        real = data_ref[pl.ds(pl.multiple_of(k * ROWS, 8), ROWS), :][:sensors].astype(BF)
        imag = data_ref[pl.ds(pl.multiple_of((k + NB) * ROWS, 8), ROWS), :][:sensors].astype(BF)
        first = jnp.concatenate([real, imag], axis=1)
        second = jnp.concatenate([imag, -real], axis=1)
        dims = (((0,), (0,)), ((), ()))
        result = lax.dot_general(
            spec[0, k], first, dims, preferred_element_type=F32
        ) + lax.dot_general(spec[1, k], second, dims, preferred_element_type=F32)
        adj_ref[pl.ds(k, PTS, stride=FREQ), :] = result[:, :NCOL]
        adj_ref[pl.ds(k + NB, PTS, stride=FREQ), :] = result[:, NCOL:]

    def five_bins(i, c):
        for j in range(5):
            one_bin(i * 5 + j)
        return c

    lax.fori_loop(0, NB // 5, five_bins, 0)
    high, low = halves(inv_ref[...])
    inv = jnp.concatenate([high, high, low], axis=1)

    def to_steps(i, c):
        values = [
            adj_ref[pl.ds(pl.multiple_of((i * 4 + j) * FREQ, 8), FREQ), :] for j in range(4)
        ]
        top, rest = halves(jnp.concatenate(values, axis=1))
        result = dot(inv, jnp.concatenate([top, rest, top], axis=0))
        for j in range(4):
            block = result[:, j * NCOL : (j + 1) * NCOL]
            for p in range(4):
                keep_ref[p, i * 4 + j] = block[8 * p : 8 * p + 8]
                give_ref[p, i * 4 + j] = block[32 + 8 * p : 40 + 8 * p].astype(BF)
        return c

    lax.fori_loop(0, PTS // 4, to_steps, 0)


def adjoint(everything, fwd, inv, spectra):
    vmem = pl.BlockSpec(memory_space=pltpu.VMEM)
    return pl.pallas_call(
        adjoint_kernel,
        in_specs=[vmem] * 3 + [pl.BlockSpec(memory_space=pl.ANY)],
        out_specs=[vmem, vmem],
        out_shape=[
            jax.ShapeDtypeStruct((4, PTS, 8, NCOL), F32),
            jax.ShapeDtypeStruct((4, PTS, 8, NCOL), BF),
        ],
        scratch_shapes=[
            pltpu.VMEM((STEPS * ROWS, NCOL), F32),
            pltpu.VMEM((FREQ * ROWS, NCOL), F32),
            pltpu.VMEM((PTS * FREQ, NCOL), F32),
            pltpu.VMEM(spectra.shape, BF),
            pltpu.SemaphoreType.DMA,
        ],
        compiler_params=pltpu.CompilerParams(vmem_limit_bytes=48 << 20),
        name="adjoint",
    )(everything, fwd, inv, spectra)


def forward_kernel(
    mine_ref, other_ref, fwd_ref, inv_ref, spec_ref, out_ref, model_ref, res_ref, spec, sem
):
    copy = pltpu.make_async_copy(spec_ref, spec, sem)
    copy.start()
    high, low = halves(fwd_ref[...])
    fwd = jnp.concatenate([high, low], axis=1)

    def to_bins(i, c):
        values = [
            jnp.concatenate(
                [ref[p, i * 4 + j].astype(F32) for ref in (mine_ref, other_ref) for p in range(4)],
                axis=0,
            ).astype(BF)
            for j in range(4)
        ]
        block = jnp.concatenate(values, axis=1)
        result = dot(fwd, jnp.concatenate([block, block], axis=0))
        for j in range(4):
            model_ref[pl.ds(i * 4 + j, FREQ, stride=PTS), :] = result[:, j * NCOL : (j + 1) * NCOL]
        return c

    lax.fori_loop(0, PTS // 4, to_bins, 0)
    copy.wait()
    sensors = spec.shape[2]
    zero = jnp.zeros((ROWS, NCOL), F32)
    for j in range(2 * NB, FREQ):
        res_ref[pl.ds(j, ROWS, stride=FREQ), :] = zero
    pad = jnp.zeros((ROWS - sensors, 2 * NCOL), F32)

    def one_bin(k):
        real = model_ref[pl.ds(pl.multiple_of(k * PTS, 8), PTS), :].astype(BF)
        imag = model_ref[pl.ds(pl.multiple_of((k + NB) * PTS, 8), PTS), :].astype(BF)
        result = dot(spec[0, k], jnp.concatenate([real, imag], axis=1)) + dot(
            spec[1, k], jnp.concatenate([-imag, real], axis=1)
        )
        result = jnp.concatenate([result, pad], axis=0)
        res_ref[pl.ds(k, ROWS, stride=FREQ), :] = result[:, :NCOL]
        res_ref[pl.ds(k + NB, ROWS, stride=FREQ), :] = result[:, NCOL:]

    def five_bins(i, c):
        for j in range(5):
            one_bin(i * 5 + j)
        return c

    lax.fori_loop(0, NB // 5, five_bins, 0)

    high, low = halves(inv_ref[...])
    inv = jnp.concatenate([high, high, low], axis=1)

    def to_steps(i, c):
        values = [
            res_ref[pl.ds(pl.multiple_of((i * 4 + j) * FREQ, 8), FREQ), :] for j in range(4)
        ]
        top, rest = halves(jnp.concatenate(values, axis=1))
        result = dot(inv, jnp.concatenate([top, rest, top], axis=0))
        for j in range(4):
            model_ref[pl.ds(i * 4 + j, STEPS, stride=ROWS), :] = result[:, j * NCOL : (j + 1) * NCOL]
        return c

    lax.fori_loop(0, ROWS // 4, to_steps, 0)
    for i in range(STEPS):
        out_ref[i] = model_ref[pl.ds(i * ROWS, ROWS), :].astype(BF)


def forward_map(mine, other, fwd, inv, spectra):
    vmem = pl.BlockSpec(memory_space=pltpu.VMEM)
    return pl.pallas_call(
        forward_kernel,
        in_specs=[vmem] * 4 + [pl.BlockSpec(memory_space=pl.ANY)],
        out_specs=vmem,
        out_shape=jax.ShapeDtypeStruct((STEPS, ROWS, NCOL), BF),
        scratch_shapes=[
            pltpu.VMEM((FREQ * PTS, NCOL), F32),
            pltpu.VMEM((ROWS * FREQ, NCOL), F32),
            pltpu.VMEM(spectra.shape, BF),
            pltpu.SemaphoreType.DMA,
        ],
        compiler_params=pltpu.CompilerParams(vmem_limit_bytes=48 << 20),
        name="forward_map",
    )(mine, other, fwd, inv, spectra)


def shards(readings, spectra, stiffness):
    yh, core = lax.axis_index("yh"), lax.axis_index("core")
    sensors = readings.shape[1]
    by_place = np.arange(STEPS).reshape(4, 8, 2).transpose(0, 2, 1).reshape(-1)
    halves_of = [np.arange(STEPS), np.roll(np.arange(STEPS), 32)]
    fwd_f = jnp.where(core == 0, *[jnp.asarray(forward_table(s)) for s in halves_of])
    inv_f = jnp.where(core == 0, *[jnp.asarray(inverse_table(s)) for s in halves_of])

    chain = [(i, i + 1) for i in range(31)]
    back = [(i + 1, i) for i in range(31)]
    swap = [(0, 1), (1, 0)]
    other = lax.ppermute(stiffness, "yh", swap)
    coeff = jnp.where(
        yh == 0, jnp.concatenate([stiffness, other]), jnp.concatenate([other, stiffness])
    )
    coeff = jnp.concatenate(
        [
            lax.ppermute(coeff[-GY:], ("x", "z"), chain),
            coeff,
            lax.ppermute(coeff[:GY], ("x", "z"), back),
        ]
    ).reshape(6, GY)

    column = jnp.pad(readings, ((0, 0), (0, ROWS - sensors), (0, 0)))
    column = lax.all_gather(column, "z", axis=0, tiled=True)
    column = jnp.broadcast_to(column[None], (8,) + column.shape).reshape(STEPS, ROWS, NCOL)
    everything = lax.all_to_all(column, ("x", "yh"), 0, 0, tiled=True)
    keep, give = adjoint(everything, jnp.asarray(forward_table(by_place)), inv_f, spectra)

    field = (keep + lax.ppermute(give, "core", swap).astype(F32)).astype(BF)
    field = lax.all_to_all(field, ("yh", "yl"), 0, 0, tiled=True).astype(F32)
    field = field.reshape(2, 2, PTS, 8, NCOL)
    grid = (field[:, 0] + field[:, 1]).reshape(4, GY, 8, NCOL)
    low = lax.ppermute(grid[-2:].astype(BF), ("x", "z"), chain)
    high = lax.ppermute(grid[:2].astype(BF), ("x", "z"), back)
    grid = jnp.concatenate([low.astype(F32), grid, high.astype(F32)])
    for sweep in range(2):
        inner = grid[1:-1]
        sides = jnp.pad(inner, ((0, 0), (1, 1), (0, 0), (0, 0)))
        beside = grid[:-2] + grid[2:] + sides[:, :-2] + sides[:, 2:]
        rows = coeff if sweep == 0 else coeff[1:-1]
        grid = inner + rows[:, :, None, None] * (beside - 4.0 * inner)
    grid = grid.astype(BF).reshape(2, 1, PTS, 8, NCOL)
    grid = jnp.broadcast_to(grid, (2, 2, PTS, 8, NCOL)).reshape(4, PTS, 8, NCOL)
    mine = lax.all_to_all(grid, ("yh", "yl"), 0, 0, tiled=True)
    other = lax.ppermute(mine, "core", swap)

    out = forward_map(mine, other, fwd_f, jnp.asarray(inverse_table(by_place)), spectra)
    out = lax.all_to_all(out, ("x", "yh"), 0, 0, tiled=True).astype(F32)
    out = jnp.sum(out.reshape(8, 8, ROWS, NCOL), axis=0).astype(BF)
    out = lax.all_to_all(out, "z", 0, 0, tiled=True).astype(F32)
    return jnp.sum(out, axis=0, keepdims=True)[:, :sensors]


def solution(mesh):
    fine = Mesh(mesh.devices.reshape(4, 8, 2, 2, 2), ("x", "z", "yh", "yl", "core"))
    param, sensor = ("x", "z", "yh"), ("yl", "core")
    return jax.shard_map(
        shards,
        mesh=fine,
        in_specs=(P(param, sensor, None), P(None, None, sensor, param), P(param)),
        out_specs=P(param, sensor, None),
        check_vma=False,
    )
```

```python
import math

import jax
import jax.numpy as jnp
from jax import lax
from jax.experimental import pallas as pl
from jax.experimental.pallas import tpu as pltpu
from jax.sharding import Mesh, PartitionSpec as P

STEPS = 64
NB = STEPS + 1
GY = 64
NCOL = 128
BF = jnp.bfloat16
F32 = jnp.float32


ROWS = 152
FREQ = 136
PTS = 128
PIECES = 8


def bins_of(shape, axis):
    row = lax.broadcasted_iota(jnp.int32, shape, axis)
    return row, jnp.where(row < NB, row, row - NB)


def forward_table(steps):
    row, bins = bins_of((FREQ, steps.shape[0]), 0)
    angle = (bins * steps[None, :] % (2 * STEPS)).astype(F32) * (2.0 * math.pi / (2 * STEPS))
    value = jnp.where(row < NB, jnp.cos(angle), -jnp.sin(angle)) * (1.0 / math.sqrt(STEPS))
    return jnp.where(row < 2 * NB, value, 0.0)


def inverse_table(steps):
    row, bins = bins_of((steps.shape[0], FREQ), 1)
    angle = (bins * steps[:, None] % (2 * STEPS)).astype(F32) * (2.0 * math.pi / (2 * STEPS))
    value = jnp.where(row < NB, jnp.cos(angle), -jnp.sin(angle)) * (1.0 / math.sqrt(STEPS))
    value = value * jnp.where((bins == 0) | (bins == STEPS), 1.0, 2.0)
    return jnp.where(row < 2 * NB, value, 0.0)


def halves(value):
    high = value.astype(BF)
    return high, (value - high.astype(F32)).astype(BF)


def dot(a, b):
    return jnp.dot(a, b, preferred_element_type=F32)


def adjoint_kernel(*refs):
    pieces = refs[:PIECES]
    fwd_ref, inv_ref, spec_ref, keep_ref, give_ref = refs[PIECES : PIECES + 5]
    time_ref, data_ref, adj_ref, spec, sem = refs[PIECES + 5 :]
    copy = pltpu.make_async_copy(spec_ref, spec, sem)
    copy.start()
    for i in range(STEPS):
        time_ref[pl.ds(i * ROWS, ROWS), :] = pieces[i // 8][i % 8].astype(F32)
    high, low = halves(fwd_ref[...])
    fwd = jnp.concatenate([high, low], axis=1)

    def to_bins(i, c):
        s0 = i * 4
        values = [time_ref[pl.ds(s0 + j, STEPS, stride=ROWS), :].astype(BF) for j in range(4)]
        block = jnp.concatenate(values, axis=1)
        result = dot(fwd, jnp.concatenate([block, block], axis=0))
        for j in range(4):
            data_ref[pl.ds(s0 + j, FREQ, stride=ROWS), :] = result[:, j * NCOL : (j + 1) * NCOL]
        return c

    lax.fori_loop(0, ROWS // 4, to_bins, 0)
    copy.wait()
    zero = jnp.zeros((PTS, NCOL), F32)
    for j in range(2 * NB, FREQ):
        adj_ref[pl.ds(j, PTS, stride=FREQ), :] = zero
    sensors = spec.shape[2]

    def one_bin(k):
        real = data_ref[pl.ds(pl.multiple_of(k * ROWS, 8), ROWS), :][:sensors].astype(BF)
        imag = data_ref[pl.ds(pl.multiple_of((k + NB) * ROWS, 8), ROWS), :][:sensors].astype(BF)
        first = jnp.concatenate([real, imag], axis=1)
        second = jnp.concatenate([imag, -real], axis=1)
        dims = (((0,), (0,)), ((), ()))
        result = lax.dot_general(
            spec[0, k], first, dims, preferred_element_type=F32
        ) + lax.dot_general(spec[1, k], second, dims, preferred_element_type=F32)
        adj_ref[pl.ds(k, PTS, stride=FREQ), :] = result[:, :NCOL]
        adj_ref[pl.ds(k + NB, PTS, stride=FREQ), :] = result[:, NCOL:]

    def five_bins(i, c):
        for j in range(5):
            one_bin(i * 5 + j)
        return c

    lax.fori_loop(0, NB // 5, five_bins, 0)
    high, low = halves(inv_ref[...])
    inv = jnp.concatenate([high, high, low], axis=1)

    def to_steps(i, c):
        values = [
            adj_ref[pl.ds(pl.multiple_of((i * 4 + j) * FREQ, 8), FREQ), :] for j in range(4)
        ]
        top, rest = halves(jnp.concatenate(values, axis=1))
        result = dot(inv, jnp.concatenate([top, rest, top], axis=0))
        for j in range(4):
            block = result[:, j * NCOL : (j + 1) * NCOL]
            for p in range(4):
                keep_ref[p, i * 4 + j] = block[8 * p : 8 * p + 8]
                give_ref[p, i * 4 + j] = block[32 + 8 * p : 40 + 8 * p].astype(BF)
        return c

    lax.fori_loop(0, PTS // 4, to_steps, 0)


def adjoint(pieces, fwd, inv, spectra):
    vmem = pl.BlockSpec(memory_space=pltpu.VMEM)
    return pl.pallas_call(
        adjoint_kernel,
        in_specs=[vmem] * (PIECES + 2) + [pl.BlockSpec(memory_space=pl.ANY)],
        out_specs=[vmem, vmem],
        out_shape=[
            jax.ShapeDtypeStruct((4, PTS, 8, NCOL), F32),
            jax.ShapeDtypeStruct((4, PTS, 8, NCOL), BF),
        ],
        scratch_shapes=[
            pltpu.VMEM((STEPS * ROWS, NCOL), F32),
            pltpu.VMEM((FREQ * ROWS, NCOL), F32),
            pltpu.VMEM((PTS * FREQ, NCOL), F32),
            pltpu.VMEM(spectra.shape, BF),
            pltpu.SemaphoreType.DMA,
        ],
        compiler_params=pltpu.CompilerParams(vmem_limit_bytes=48 << 20),
        name="adjoint",
    )(*pieces, fwd, inv, spectra)


def forward_kernel(*refs):
    model_in, (fwd_ref, inv_ref, spec_ref) = refs[:5], refs[5:8]
    outs, (model_ref, res_ref, spec, sem) = refs[8 : 8 + PIECES], refs[8 + PIECES :]
    copy = pltpu.make_async_copy(spec_ref, spec, sem)
    copy.start()
    high, low = halves(fwd_ref[...])
    fwd = jnp.concatenate([high, low], axis=1)

    def to_bins(i, c):
        values = [
            jnp.concatenate(
                [ref[i * 4 + j].astype(F32) for ref in model_in[:4]]
                + [model_in[4][p, i * 4 + j].astype(F32) for p in range(4)],
                axis=0,
            ).astype(BF)
            for j in range(4)
        ]
        block = jnp.concatenate(values, axis=1)
        result = dot(fwd, jnp.concatenate([block, block], axis=0))
        for j in range(4):
            model_ref[pl.ds(i * 4 + j, FREQ, stride=PTS), :] = result[:, j * NCOL : (j + 1) * NCOL]
        return c

    lax.fori_loop(0, PTS // 4, to_bins, 0)
    copy.wait()
    sensors = spec.shape[2]
    zero = jnp.zeros((ROWS, NCOL), F32)
    for j in range(2 * NB, FREQ):
        res_ref[pl.ds(j, ROWS, stride=FREQ), :] = zero
    pad = jnp.zeros((ROWS - sensors, 2 * NCOL), F32)

    def one_bin(k):
        real = model_ref[pl.ds(pl.multiple_of(k * PTS, 8), PTS), :].astype(BF)
        imag = model_ref[pl.ds(pl.multiple_of((k + NB) * PTS, 8), PTS), :].astype(BF)
        result = dot(spec[0, k], jnp.concatenate([real, imag], axis=1)) + dot(
            spec[1, k], jnp.concatenate([-imag, real], axis=1)
        )
        result = jnp.concatenate([result, pad], axis=0)
        res_ref[pl.ds(k, ROWS, stride=FREQ), :] = result[:, :NCOL]
        res_ref[pl.ds(k + NB, ROWS, stride=FREQ), :] = result[:, NCOL:]

    def five_bins(i, c):
        for j in range(5):
            one_bin(i * 5 + j)
        return c

    lax.fori_loop(0, NB // 5, five_bins, 0)

    high, low = halves(inv_ref[...])
    inv = jnp.concatenate([high, high, low], axis=1)

    def to_steps(i, c):
        values = [
            res_ref[pl.ds(pl.multiple_of((i * 4 + j) * FREQ, 8), FREQ), :] for j in range(4)
        ]
        top, rest = halves(jnp.concatenate(values, axis=1))
        result = dot(inv, jnp.concatenate([top, rest, top], axis=0))
        for j in range(4):
            model_ref[pl.ds(i * 4 + j, STEPS, stride=ROWS), :] = result[:, j * NCOL : (j + 1) * NCOL]
        return c

    lax.fori_loop(0, ROWS // 4, to_steps, 0)
    for i in range(STEPS):
        ref = outs[i // 8]
        ref[i % 8] = model_ref[pl.ds(i * ROWS, ROWS), :].astype(ref.dtype)


def forward_map(mine, other, fwd, inv, spectra):
    vmem = pl.BlockSpec(memory_space=pltpu.VMEM)
    return pl.pallas_call(
        forward_kernel,
        in_specs=[vmem] * 7 + [pl.BlockSpec(memory_space=pl.ANY)],
        out_specs=[vmem] * PIECES,
        out_shape=[
            jax.ShapeDtypeStruct((8, ROWS, NCOL), F32 if i == 0 else BF) for i in range(PIECES)
        ],
        scratch_shapes=[
            pltpu.VMEM((FREQ * PTS, NCOL), F32),
            pltpu.VMEM((ROWS * FREQ, NCOL), F32),
            pltpu.VMEM(spectra.shape, BF),
            pltpu.SemaphoreType.DMA,
        ],
        compiler_params=pltpu.CompilerParams(vmem_limit_bytes=48 << 20),
        name="forward_map",
    )(*mine, other, fwd, inv, spectra)


def from_z(v, d):
    return lax.ppermute(v, "z", [((i + d) % 8, i) for i in range(8)])


def flip(v, *axes):
    size = 2 ** len(axes)
    return lax.ppermute(v, axes, [(i, size - 1 - i) for i in range(size)])


def xy_pairs(dx, dy):
    return [
        (2 * x + y, 2 * ((x + dx) % 4) + (y ^ dy)) for x in range(4) for y in range(2)
    ]


PLACES = tuple((dx, dy) for dx in range(4) for dy in range(2))


def shards(readings, spectra, stiffness):
    x, z, yh = lax.axis_index("x"), lax.axis_index("z"), lax.axis_index("yh")
    yl, core = lax.axis_index("yl"), lax.axis_index("core")
    sensors = readings.shape[1]
    i = jnp.arange(STEPS, dtype=jnp.int32)
    steps = (
        (x + i // 16) % 4 * 16 + ((z + i // 2 % 4 * 2) % 8 ^ (i % 2)) * 2 + (yh ^ (i // 8 % 2))
    )
    steps_f = ((core ^ (i // 32)) * 4 + (yh ^ (i // 16 % 2)) * 2 + (yl ^ (i // 8 % 2))) * 8 + i % 8

    chain = [(i, i + 1) for i in range(31)]
    back = [(i + 1, i) for i in range(31)]
    other = flip(stiffness, "yh")
    coeff = jnp.where(
        yh == 0, jnp.concatenate([stiffness, other]), jnp.concatenate([other, stiffness])
    )
    coeff = jnp.concatenate(
        [
            lax.ppermute(coeff[-GY:], ("x", "z"), chain),
            coeff,
            lax.ppermute(coeff[:GY], ("x", "z"), back),
        ]
    ).reshape(6, GY)

    column = jnp.pad(readings, ((0, 0), (0, ROWS - sensors), (0, 0)))
    column = jnp.concatenate(
        [column, lax.ppermute(column, "z", [(i, i ^ 1) for i in range(8)])]
    )
    column = jnp.concatenate([column] + [from_z(column, 2 * d) for d in (1, 2, 3)])
    pieces = [column] + [
        lax.ppermute(column, ("x", "yh"), [(s, d) for d, s in xy_pairs(dx, dy)])
        for dx, dy in PLACES[1:]
    ]
    pieces, coeff = lax.optimization_barrier((pieces, coeff))
    keep, give = adjoint(pieces, forward_table(steps), inverse_table(steps_f), spectra)

    field = keep + flip(give, "core").astype(F32)
    here = field[0] + flip(field[1].astype(BF), "yl").astype(F32)
    there = flip(field[2].astype(BF), "yh").astype(F32) + flip(
        field[3].astype(BF), "yh", "yl"
    ).astype(F32)
    here, there = here.reshape(2, GY, 8, NCOL), there.reshape(2, GY, 8, NCOL)
    grid = jnp.where(yh == 0, jnp.concatenate([here, there]), jnp.concatenate([there, here]))
    low = lax.ppermute(grid[-2:].astype(BF), ("x", "z"), chain)
    high = lax.ppermute(grid[:2].astype(BF), ("x", "z"), back)
    grid = jnp.concatenate([low.astype(F32), grid, high.astype(F32)])
    for sweep in range(2):
        inner = grid[1:-1]
        sides = jnp.pad(inner, ((0, 0), (1, 1), (0, 0), (0, 0)))
        beside = grid[:-2] + grid[2:] + sides[:, :-2] + sides[:, 2:]
        rows = coeff if sweep == 0 else coeff[1:-1]
        grid = inner + rows[:, :, None, None] * (beside - 4.0 * inner)
    grid = grid.astype(BF).reshape(2, PTS, 8, NCOL)
    here = jnp.where(yh == 0, grid[0], grid[1])
    there = jnp.where(yh == 0, grid[1], grid[0])
    mine = [here, flip(here, "yl"), flip(there, "yh"), flip(there, "yh", "yl")]
    other = flip(jnp.stack(mine), "core")

    outs = forward_map(mine, other, forward_table(steps_f), inverse_table(steps), spectra)
    total = outs[0]
    parts = [
        lax.ppermute(part, ("x", "yh"), xy_pairs(dx, dy))
        for (dx, dy), part in zip(PLACES[1:], outs[1:])
    ]
    for part in parts:
        total = total + part.astype(F32)
    pair = total[:2]
    parts = [from_z(total[2 * d : 2 * d + 2].astype(BF), -2 * d) for d in (1, 2, 3)]
    for part in parts:
        pair = pair + part.astype(F32)
    last = lax.ppermute(pair[1:], "z", [(i, i ^ 1) for i in range(8)])
    return (pair[:1] + last)[:, :sensors]


def solution(mesh):
    fine = Mesh(mesh.devices.reshape(4, 8, 2, 2, 2), ("x", "z", "yh", "yl", "core"))
    param, sensor = ("x", "z", "yh"), ("yl", "core")
    return jax.shard_map(
        shards,
        mesh=fine,
        in_specs=(P(param, sensor, None), P(None, None, sensor, param), P(param)),
        out_specs=P(param, sensor, None),
        check_vma=False,
    )
```

```python
import math

import jax
import jax.numpy as jnp
from jax import lax
from jax.experimental import pallas as pl
from jax.experimental.pallas import tpu as pltpu
from jax.sharding import Mesh, PartitionSpec as P

STEPS = 64
NB = STEPS + 1
GY = 64
NCOL = 128
BF = jnp.bfloat16
F32 = jnp.float32


ROWS = 152
FREQ = 136
PTS = 128
BY_SENSOR = 153
BY_BIN = 137
BY_POINT = 129
PIECE_STEPS = (8, 8, 4, 4, 8) * 2
PIECES = len(PIECE_STEPS)


def bins_of(shape, axis):
    row = lax.broadcasted_iota(jnp.int32, shape, axis)
    return row, jnp.where(row < NB, row, row - NB)


def forward_table(steps):
    row, bins = bins_of((FREQ, steps.shape[0]), 0)
    angle = (bins * steps[None, :] % (2 * STEPS)).astype(F32) * (2.0 * math.pi / (2 * STEPS))
    value = jnp.where(row < NB, jnp.cos(angle), -jnp.sin(angle)) * (1.0 / math.sqrt(STEPS))
    return jnp.where(row < 2 * NB, value, 0.0)


def inverse_table(steps):
    row, bins = bins_of((steps.shape[0], FREQ), 1)
    angle = (bins * steps[:, None] % (2 * STEPS)).astype(F32) * (2.0 * math.pi / (2 * STEPS))
    value = jnp.where(row < NB, jnp.cos(angle), -jnp.sin(angle)) * (1.0 / math.sqrt(STEPS))
    value = value * jnp.where((bins == 0) | (bins == STEPS), 1.0, 2.0)
    return jnp.where(row < 2 * NB, value, 0.0)


def rows_at(index, stride, count):
    return pl.ds(index * stride, count)


def halves(value):
    high = value.astype(BF)
    return high, (value - high.astype(F32)).astype(BF)


def dot(a, b):
    return jnp.dot(a, b, preferred_element_type=F32)


def adjoint_kernel(*refs):
    pieces = refs[:PIECES]
    fwd_ref, inv_ref, spec_ref, keep_ref, give_ref = refs[PIECES : PIECES + 5]
    time_ref, data_ref, adj_ref, spec, sem = refs[PIECES + 5 :]
    copy = pltpu.make_async_copy(spec_ref, spec, sem)
    copy.start()
    i = 0
    for ref in pieces:
        for j in range(ref.shape[0]):
            time_ref[pl.ds(i * BY_SENSOR, ROWS), :] = ref[j].astype(F32)
            i += 1
    high, low = halves(fwd_ref[...])
    fwd = jnp.concatenate([high, low], axis=1)

    def to_bins(i, c):
        s0 = i * 4
        values = [time_ref[pl.ds(s0 + j, STEPS, stride=BY_SENSOR), :].astype(BF) for j in range(4)]
        block = jnp.concatenate(values, axis=1)
        result = dot(fwd, jnp.concatenate([block, block], axis=0))
        for j in range(4):
            data_ref[pl.ds(s0 + j, FREQ, stride=BY_SENSOR), :] = result[:, j * NCOL : (j + 1) * NCOL]
        return c

    lax.fori_loop(0, ROWS // 4, to_bins, 0)
    copy.wait()
    zero = jnp.zeros((PTS, NCOL), F32)
    for j in range(2 * NB, FREQ):
        adj_ref[pl.ds(j, PTS, stride=BY_BIN), :] = zero
    sensors = spec.shape[2]

    def one_bin(k):
        real = data_ref[rows_at(k, BY_SENSOR, ROWS), :][:sensors].astype(BF)
        imag = data_ref[rows_at(k + NB, BY_SENSOR, ROWS), :][:sensors].astype(BF)
        first = jnp.concatenate([real, imag], axis=1)
        second = jnp.concatenate([imag, -real], axis=1)
        dims = (((0,), (0,)), ((), ()))
        result = lax.dot_general(
            spec[0, k], first, dims, preferred_element_type=F32
        ) + lax.dot_general(spec[1, k], second, dims, preferred_element_type=F32)
        adj_ref[pl.ds(k, PTS, stride=BY_BIN), :] = result[:, :NCOL]
        adj_ref[pl.ds(k + NB, PTS, stride=BY_BIN), :] = result[:, NCOL:]

    def five_bins(i, c):
        for j in range(5):
            one_bin(i * 5 + j)
        return c

    lax.fori_loop(0, NB // 5, five_bins, 0)
    high, low = halves(inv_ref[...])
    inv = jnp.concatenate([high, high, low], axis=1)

    def to_steps(i, c):
        values = [
            adj_ref[rows_at(i * 4 + j, BY_BIN, FREQ), :] for j in range(4)
        ]
        top, rest = halves(jnp.concatenate(values, axis=1))
        result = dot(inv, jnp.concatenate([top, rest, top], axis=0))
        for j in range(4):
            block = result[:, j * NCOL : (j + 1) * NCOL]
            for p in range(4):
                keep_ref[p, i * 4 + j] = block[8 * p : 8 * p + 8]
                give_ref[p, i * 4 + j] = block[32 + 8 * p : 40 + 8 * p].astype(BF)
        return c

    lax.fori_loop(0, PTS // 4, to_steps, 0)


def adjoint(pieces, fwd, inv, spectra):
    vmem = pl.BlockSpec(memory_space=pltpu.VMEM)
    return pl.pallas_call(
        adjoint_kernel,
        in_specs=[vmem] * (PIECES + 2) + [pl.BlockSpec(memory_space=pl.ANY)],
        out_specs=[vmem, vmem],
        out_shape=[
            jax.ShapeDtypeStruct((4, PTS, 8, NCOL), F32),
            jax.ShapeDtypeStruct((4, PTS, 8, NCOL), BF),
        ],
        scratch_shapes=[
            pltpu.VMEM((STEPS * BY_SENSOR, NCOL), F32),
            pltpu.VMEM((FREQ * BY_SENSOR, NCOL), F32),
            pltpu.VMEM((PTS * BY_BIN, NCOL), F32),
            pltpu.VMEM(spectra.shape, BF),
            pltpu.SemaphoreType.DMA,
        ],
        compiler_params=pltpu.CompilerParams(vmem_limit_bytes=48 << 20),
        name="adjoint",
    )(*pieces, fwd, inv, spectra)


def forward_kernel(*refs):
    model_in, (fwd_ref, inv_ref, spec_ref) = refs[:5], refs[5:8]
    outs, (model_ref, res_ref, spec, sem) = refs[8 : 8 + PIECES], refs[8 + PIECES :]
    copy = pltpu.make_async_copy(spec_ref, spec, sem)
    copy.start()
    high, low = halves(fwd_ref[...])
    fwd = jnp.concatenate([high, low], axis=1)

    def to_bins(i, c):
        values = [
            jnp.concatenate(
                [ref[i * 4 + j].astype(F32) for ref in model_in[:4]]
                + [model_in[4][p, i * 4 + j].astype(F32) for p in range(4)],
                axis=0,
            ).astype(BF)
            for j in range(4)
        ]
        block = jnp.concatenate(values, axis=1)
        result = dot(fwd, jnp.concatenate([block, block], axis=0))
        for j in range(4):
            model_ref[pl.ds(i * 4 + j, FREQ, stride=BY_POINT), :] = result[:, j * NCOL : (j + 1) * NCOL]
        return c

    lax.fori_loop(0, PTS // 4, to_bins, 0)
    copy.wait()
    sensors = spec.shape[2]
    zero = jnp.zeros((ROWS, NCOL), F32)
    for j in range(2 * NB, FREQ):
        res_ref[pl.ds(j, ROWS, stride=BY_BIN), :] = zero
    pad = jnp.zeros((ROWS - sensors, 2 * NCOL), F32)

    def one_bin(k):
        real = model_ref[rows_at(k, BY_POINT, PTS), :].astype(BF)
        imag = model_ref[rows_at(k + NB, BY_POINT, PTS), :].astype(BF)
        result = dot(spec[0, k], jnp.concatenate([real, imag], axis=1)) + dot(
            spec[1, k], jnp.concatenate([-imag, real], axis=1)
        )
        result = jnp.concatenate([result, pad], axis=0)
        res_ref[pl.ds(k, ROWS, stride=BY_BIN), :] = result[:, :NCOL]
        res_ref[pl.ds(k + NB, ROWS, stride=BY_BIN), :] = result[:, NCOL:]

    def five_bins(i, c):
        for j in range(5):
            one_bin(i * 5 + j)
        return c

    lax.fori_loop(0, NB // 5, five_bins, 0)

    high, low = halves(inv_ref[...])
    inv = jnp.concatenate([high, high, low], axis=1)

    def to_steps(i, c):
        values = [
            res_ref[rows_at(i * 4 + j, BY_BIN, FREQ), :] for j in range(4)
        ]
        top, rest = halves(jnp.concatenate(values, axis=1))
        result = dot(inv, jnp.concatenate([top, rest, top], axis=0))
        for j in range(4):
            model_ref[pl.ds(i * 4 + j, STEPS, stride=BY_SENSOR), :] = result[:, j * NCOL : (j + 1) * NCOL]
        return c

    lax.fori_loop(0, ROWS // 4, to_steps, 0)
    i = 0
    for ref in outs:
        for j in range(ref.shape[0]):
            ref[j] = model_ref[pl.ds(i * BY_SENSOR, ROWS), :].astype(ref.dtype)
            i += 1


def forward_map(mine, other, fwd, inv, spectra):
    vmem = pl.BlockSpec(memory_space=pltpu.VMEM)
    return pl.pallas_call(
        forward_kernel,
        in_specs=[vmem] * 7 + [pl.BlockSpec(memory_space=pl.ANY)],
        out_specs=[vmem] * PIECES,
        out_shape=[
            jax.ShapeDtypeStruct((count, ROWS, NCOL), BF if count == 4 else F32)
            for count in PIECE_STEPS
        ],
        scratch_shapes=[
            pltpu.VMEM((FREQ * BY_POINT, NCOL), F32),
            pltpu.VMEM((ROWS * BY_BIN, NCOL), F32),
            pltpu.VMEM(spectra.shape, BF),
            pltpu.SemaphoreType.DMA,
        ],
        compiler_params=pltpu.CompilerParams(vmem_limit_bytes=48 << 20),
        name="forward_map",
    )(*mine, other, fwd, inv, spectra)


def from_z(v, d):
    return lax.ppermute(v, "z", [((i + d) % 8, i) for i in range(8)])


def from_x(v, d):
    return lax.ppermute(v, "x", [((i + d) % 4, i) for i in range(4)])


def flip(v, *axes):
    size = 2 ** len(axes)
    return lax.ppermute(v, axes, [(i, size - 1 - i) for i in range(size)])


def shards(readings, spectra, stiffness):
    x, z, yh = lax.axis_index("x"), lax.axis_index("z"), lax.axis_index("yh")
    yl, core = lax.axis_index("yl"), lax.axis_index("core")
    sensors = readings.shape[1]
    i = jnp.arange(STEPS, dtype=jnp.int32)
    steps = (
        (x + i // 8) % 4 * 16 + ((z + i // 2 % 4 * 2) % 8 ^ (i % 2)) * 2 + (yh ^ (i // 32))
    )
    steps_f = ((core ^ (i // 32)) * 4 + (yh ^ (i // 16 % 2)) * 2 + (yl ^ (i // 8 % 2))) * 8 + i % 8

    column = jnp.pad(readings, ((0, 0), (0, ROWS - sensors), (0, 0)))
    column = jnp.concatenate(
        [column, lax.ppermute(column, "z", [(i, i ^ 1) for i in range(8)])]
    )
    column = jnp.concatenate([column] + [from_z(column, 2 * d) for d in (1, 2, 3)])
    column, stiffness = lax.optimization_barrier((column, stiffness))
    up, down, across = from_x(column, 1), from_x(column, -1), flip(column, "yh")
    far = [from_x(up[:4], 1), from_x(down[4:], -1)]
    pieces = [column, up] + far + [down]
    up, down = from_x(across, 1), from_x(across, -1)
    far = [from_x(up[:4], 1), from_x(down[4:], -1)]
    pieces += [across, up] + far + [down]

    chain = [(i, i + 1) for i in range(31)]
    back = [(i + 1, i) for i in range(31)]
    other = flip(stiffness, "yh")
    coeff = jnp.where(
        yh == 0, jnp.concatenate([stiffness, other]), jnp.concatenate([other, stiffness])
    )
    coeff = jnp.concatenate(
        [
            lax.ppermute(coeff[-GY:], ("x", "z"), chain),
            coeff,
            lax.ppermute(coeff[:GY], ("x", "z"), back),
        ]
    ).reshape(6, GY)

    pieces, coeff = lax.optimization_barrier((pieces, coeff))
    keep, give = adjoint(pieces, forward_table(steps), inverse_table(steps_f), spectra)

    field = keep + flip(give, "core").astype(F32)
    here = field[0] + flip(field[1].astype(BF), "yl").astype(F32)
    there = flip(field[2].astype(BF), "yh").astype(F32) + flip(
        field[3].astype(BF), "yh", "yl"
    ).astype(F32)
    here, there = here.reshape(2, GY, 8, NCOL), there.reshape(2, GY, 8, NCOL)
    grid = jnp.where(yh == 0, jnp.concatenate([here, there]), jnp.concatenate([there, here]))
    low = lax.ppermute(grid[-2:].astype(BF), ("x", "z"), chain)
    high = lax.ppermute(grid[:2].astype(BF), ("x", "z"), back)
    grid = jnp.concatenate([low.astype(F32), grid, high.astype(F32)])
    for sweep in range(2):
        inner = grid[1:-1]
        sides = jnp.pad(inner, ((0, 0), (1, 1), (0, 0), (0, 0)))
        beside = grid[:-2] + grid[2:] + sides[:, :-2] + sides[:, 2:]
        rows = coeff if sweep == 0 else coeff[1:-1]
        grid = inner + rows[:, :, None, None] * (beside - 4.0 * inner)
    grid = grid.astype(BF).reshape(2, PTS, 8, NCOL)
    here = jnp.where(yh == 0, grid[0], grid[1])
    there = jnp.where(yh == 0, grid[1], grid[0])
    mine = [here, flip(here, "yl"), flip(there, "yh"), flip(there, "yh", "yl")]
    other = flip(jnp.stack(mine), "core")

    outs = forward_map(mine, other, forward_table(steps_f), inverse_table(steps), spectra)
    near, back_across = outs[:5], outs[5:]

    def far_first(parts):
        low, high = from_x(parts[2], -1).astype(F32), from_x(parts[3], 1).astype(F32)
        up = jnp.concatenate([parts[1][:4] + low, parts[1][4:]]).astype(BF)
        down = jnp.concatenate([parts[4][:4], parts[4][4:] + high]).astype(BF)
        return up, down

    def gather_up(parts, up, down):
        return parts[0] + from_x(up, -1).astype(F32) + from_x(down, 1).astype(F32)

    across = gather_up(back_across, *far_first(back_across)).astype(BF)
    up, down = far_first(near)
    total = gather_up(near, up, down) + flip(across, "yh").astype(F32)
    pair = total[:2]
    parts = [from_z(total[2 * d : 2 * d + 2].astype(BF), -2 * d) for d in (1, 2, 3)]
    for part in parts:
        pair = pair + part.astype(F32)
    last = lax.ppermute(pair[1:], "z", [(i, i ^ 1) for i in range(8)])
    return (pair[:1] + last)[:, :sensors]


def solution(mesh):
    fine = Mesh(mesh.devices.reshape(4, 8, 2, 2, 2), ("x", "z", "yh", "yl", "core"))
    param, sensor = ("x", "z", "yh"), ("yl", "core")
    return jax.shard_map(
        shards,
        mesh=fine,
        in_specs=(P(param, sensor, None), P(None, None, sensor, param), P(param)),
        out_specs=P(param, sensor, None),
        check_vma=False,
    )
```

```python
import math

import jax
import jax.numpy as jnp
from jax import lax
from jax.experimental import pallas as pl
from jax.experimental.pallas import tpu as pltpu
from jax.sharding import Mesh, PartitionSpec as P

STEPS = 64
NB = STEPS + 1
GY = 64
NCOL = 128
BF = jnp.bfloat16
F32 = jnp.float32


ROWS = 152
FREQ = 128
IMAG = NB - 1
PTS = 128
BY_SENSOR = 153
BY_BIN = 129
BY_POINT = 129
ROW_GROUP = 76
POINT_GROUP = 64
BINS = 63
PIECE_STEPS = (8, 8, 4, 4, 8) * 2
PIECES = len(PIECE_STEPS)


def bins_of(shape, axis):
    row = lax.broadcasted_iota(jnp.int32, shape, axis)
    return row, jnp.where(row < NB, row, row - IMAG)


def forward_table(steps):
    row, bins = bins_of((FREQ, steps.shape[0]), 0)
    angle = (bins * steps[None, :] % (2 * STEPS)).astype(F32) * (2.0 * math.pi / (2 * STEPS))
    return jnp.where(row < NB, jnp.cos(angle), -jnp.sin(angle)) * (1.0 / math.sqrt(STEPS))


def inverse_table(steps):
    row, bins = bins_of((steps.shape[0], FREQ), 1)
    angle = (bins * steps[:, None] % (2 * STEPS)).astype(F32) * (2.0 * math.pi / (2 * STEPS))
    value = jnp.where(row < NB, jnp.cos(angle), -jnp.sin(angle)) * (1.0 / math.sqrt(STEPS))
    return value * jnp.where((bins == 0) | (bins == STEPS), 1.0, 2.0)


def rows_at(index, stride, count):
    return pl.ds(index * stride, count)


def halves(value):
    high = value.astype(BF)
    return high, (value - high.astype(F32)).astype(BF)


def dot(a, b):
    return jnp.dot(a, b, preferred_element_type=F32)


def adjoint_kernel(*refs):
    pieces = refs[:PIECES]
    fwd_ref, inv_ref, spec_ref, keep_ref, give_ref = refs[PIECES : PIECES + 5]
    adj_ref, data_ref, spec, sem = refs[PIECES + 5 :]
    time_ref = adj_ref
    copy = pltpu.make_async_copy(spec_ref, spec, sem)
    copy.start()
    i = 0
    for ref in pieces:
        for j in range(ref.shape[0]):
            time_ref[pl.ds(i * BY_SENSOR, ROWS), :] = ref[j].astype(F32)
            i += 1
    high, low = halves(fwd_ref[...])
    fwd = jnp.concatenate([high, low], axis=1)

    def to_bins(i, c):
        s0 = i * ROW_GROUP
        values = [time_ref[pl.ds(s0 + j, STEPS, stride=BY_SENSOR), :].astype(BF) for j in range(ROW_GROUP)]
        block = jnp.concatenate(values, axis=1)
        result = dot(fwd, jnp.concatenate([block, block], axis=0))
        for j in range(ROW_GROUP):
            data_ref[pl.ds(s0 + j, FREQ, stride=BY_SENSOR), :] = result[:, j * NCOL : (j + 1) * NCOL]
        return c

    lax.fori_loop(0, ROWS // ROW_GROUP, to_bins, 0)
    copy.wait()
    sensors = spec.shape[2]

    dims = (((0,), (0,)), ((), ()))
    for k in (0, STEPS):
        real = data_ref[rows_at(k, BY_SENSOR, ROWS), :][:sensors].astype(BF)
        result = lax.dot_general(spec[0, k], real, dims, preferred_element_type=F32)
        adj_ref[pl.ds(k, PTS, stride=BY_BIN), :] = result

    def one_bin(k):
        real = data_ref[rows_at(k, BY_SENSOR, ROWS), :][:sensors].astype(BF)
        imag = data_ref[rows_at(k + IMAG, BY_SENSOR, ROWS), :][:sensors].astype(BF)
        first = jnp.concatenate([real, imag], axis=1)
        second = jnp.concatenate([imag, -real], axis=1)
        result = lax.dot_general(
            spec[0, k], first, dims, preferred_element_type=F32
        ) + lax.dot_general(spec[1, k], second, dims, preferred_element_type=F32)
        adj_ref[pl.ds(k, PTS, stride=BY_BIN), :] = result[:, :NCOL]
        adj_ref[pl.ds(k + IMAG, PTS, stride=BY_BIN), :] = result[:, NCOL:]

    def some_bins(i, c):
        for j in range(BINS):
            one_bin(1 + i * BINS + j)
        return c

    lax.fori_loop(0, (STEPS - 1) // BINS, some_bins, 0)
    high, low = halves(inv_ref[...])
    inv = jnp.concatenate([high, low], axis=1)

    def to_steps(i, c):
        values = [
            adj_ref[rows_at(i * POINT_GROUP + j, BY_BIN, FREQ), :] for j in range(POINT_GROUP)
        ]
        whole = jnp.concatenate(values, axis=1).astype(BF)
        result = dot(inv, jnp.concatenate([whole, whole], axis=0))
        for j in range(POINT_GROUP):
            block = result[:, j * NCOL : (j + 1) * NCOL]
            for p in range(4):
                keep_ref[p, i * POINT_GROUP + j] = block[8 * p : 8 * p + 8]
                give_ref[p, i * POINT_GROUP + j] = block[32 + 8 * p : 40 + 8 * p].astype(BF)
        return c

    lax.fori_loop(0, PTS // POINT_GROUP, to_steps, 0)


def adjoint(pieces, fwd, inv, spectra):
    vmem = pl.BlockSpec(memory_space=pltpu.VMEM)
    return pl.pallas_call(
        adjoint_kernel,
        in_specs=[vmem] * (PIECES + 2) + [pl.BlockSpec(memory_space=pl.ANY)],
        out_specs=[vmem, vmem],
        out_shape=[
            jax.ShapeDtypeStruct((4, PTS, 8, NCOL), F32),
            jax.ShapeDtypeStruct((4, PTS, 8, NCOL), BF),
        ],
        scratch_shapes=[
            pltpu.VMEM((PTS * BY_BIN, NCOL), F32),
            pltpu.VMEM((FREQ * BY_SENSOR, NCOL), F32),
            pltpu.VMEM(spectra.shape, BF),
            pltpu.SemaphoreType.DMA,
        ],
        compiler_params=pltpu.CompilerParams(vmem_limit_bytes=27 << 20),
        name="adjoint",
    )(*pieces, fwd, inv, spectra)


def forward_kernel(*refs):
    model_in, (fwd_ref, inv_ref, spec_ref) = refs[:5], refs[5:8]
    outs, (model_ref, res_ref, spec, sem) = refs[8 : 8 + PIECES], refs[8 + PIECES :]
    copy = pltpu.make_async_copy(spec_ref, spec, sem)
    copy.start()
    high, low = halves(fwd_ref[...])
    fwd = jnp.concatenate([high, low], axis=1)

    def to_bins(i, c):
        values = [
            jnp.concatenate(
                [ref[i * POINT_GROUP + j].astype(F32) for ref in model_in[:4]]
                + [model_in[4][p, i * POINT_GROUP + j].astype(F32) for p in range(4)],
                axis=0,
            ).astype(BF)
            for j in range(POINT_GROUP)
        ]
        block = jnp.concatenate(values, axis=1)
        result = dot(fwd, jnp.concatenate([block, block], axis=0))
        for j in range(POINT_GROUP):
            model_ref[pl.ds(i * POINT_GROUP + j, FREQ, stride=BY_POINT), :] = result[:, j * NCOL : (j + 1) * NCOL]
        return c

    lax.fori_loop(0, PTS // POINT_GROUP, to_bins, 0)
    copy.wait()
    sensors = spec.shape[2]
    pad = jnp.zeros((ROWS - sensors, 2 * NCOL), F32)
    for k in (0, STEPS):
        real = model_ref[rows_at(k, BY_POINT, PTS), :].astype(BF)
        result = jnp.concatenate([dot(spec[0, k], real), pad[:, :NCOL]], axis=0)
        res_ref[pl.ds(k, ROWS, stride=BY_BIN), :] = result

    def one_bin(k):
        real = model_ref[rows_at(k, BY_POINT, PTS), :].astype(BF)
        imag = model_ref[rows_at(k + IMAG, BY_POINT, PTS), :].astype(BF)
        result = dot(spec[0, k], jnp.concatenate([real, imag], axis=1)) + dot(
            spec[1, k], jnp.concatenate([-imag, real], axis=1)
        )
        result = jnp.concatenate([result, pad], axis=0)
        res_ref[pl.ds(k, ROWS, stride=BY_BIN), :] = result[:, :NCOL]
        res_ref[pl.ds(k + IMAG, ROWS, stride=BY_BIN), :] = result[:, NCOL:]

    def some_bins(i, c):
        for j in range(BINS):
            one_bin(1 + i * BINS + j)
        return c

    lax.fori_loop(0, (STEPS - 1) // BINS, some_bins, 0)

    high, low = halves(inv_ref[...])
    inv = jnp.concatenate([high, low], axis=1)

    def to_steps(i, c):
        values = [
            res_ref[rows_at(i * ROW_GROUP + j, BY_BIN, FREQ), :] for j in range(ROW_GROUP)
        ]
        whole = jnp.concatenate(values, axis=1).astype(BF)
        result = dot(inv, jnp.concatenate([whole, whole], axis=0))
        for j in range(ROW_GROUP):
            model_ref[pl.ds(i * ROW_GROUP + j, STEPS, stride=BY_SENSOR), :] = result[:, j * NCOL : (j + 1) * NCOL]
        return c

    lax.fori_loop(0, ROWS // ROW_GROUP, to_steps, 0)
    i = 0
    for ref in outs:
        for j in range(ref.shape[0]):
            ref[j] = model_ref[pl.ds(i * BY_SENSOR, ROWS), :].astype(ref.dtype)
            i += 1


def forward_map(mine, other, fwd, inv, spectra):
    vmem = pl.BlockSpec(memory_space=pltpu.VMEM)
    return pl.pallas_call(
        forward_kernel,
        in_specs=[vmem] * 7 + [pl.BlockSpec(memory_space=pl.ANY)],
        out_specs=[vmem] * PIECES,
        out_shape=[
            jax.ShapeDtypeStruct((count, ROWS, NCOL), BF if count == 4 else F32)
            for count in PIECE_STEPS
        ],
        scratch_shapes=[
            pltpu.VMEM((FREQ * BY_POINT, NCOL), F32),
            pltpu.VMEM((ROWS * BY_BIN, NCOL), F32),
            pltpu.VMEM(spectra.shape, BF),
            pltpu.SemaphoreType.DMA,
        ],
        compiler_params=pltpu.CompilerParams(vmem_limit_bytes=27 << 20),
        name="forward_map",
    )(*mine, other, fwd, inv, spectra)


def from_z(v, d):
    return lax.ppermute(v, "z", [((i + d) % 8, i) for i in range(8)])


def from_x(v, d):
    return lax.ppermute(v, "x", [((i + d) % 4, i) for i in range(4)])


def flip(v, *axes):
    size = 2 ** len(axes)
    return lax.ppermute(v, axes, [(i, size - 1 - i) for i in range(size)])


def shards(readings, spectra, stiffness):
    x, z, yh = lax.axis_index("x"), lax.axis_index("z"), lax.axis_index("yh")
    yl, core = lax.axis_index("yl"), lax.axis_index("core")
    sensors = readings.shape[1]
    i = jnp.arange(STEPS, dtype=jnp.int32)
    steps = (
        (x + i // 8) % 4 * 16 + ((z + i // 2 % 4 * 2) % 8 ^ (i % 2)) * 2 + (yh ^ (i // 32))
    )
    steps_f = ((core ^ (i // 32)) * 4 + (yh ^ (i // 16 % 2)) * 2 + (yl ^ (i // 8 % 2))) * 8 + i % 8

    high = lax.reduce_precision(stiffness, 8, 7)
    column = jnp.concatenate(
        [readings, high.astype(BF)[None, None], (stiffness - high).astype(BF)[None, None]], axis=1
    )
    column = jnp.concatenate(
        [column, lax.ppermute(column, "z", [(i, i ^ 1) for i in range(8)])]
    )
    column = jnp.concatenate([column] + [from_z(column, 2 * d) for d in (1, 2, 3)])
    up, down, across = from_x(column, 1), from_x(column, -1), flip(column, "yh")
    far = [from_x(up[:4], 1), from_x(down[4:], -1)]
    pieces = [column, up] + far + [down]
    up, down = from_x(across, 1), from_x(across, -1)
    far = [from_x(up[:4], 1), from_x(down[4:], -1)]
    pieces += [across, up] + far + [down]

    wanted = [(p + q, entry) for q in (0, 5) for p, entry in ((0, 1), (0, 7), (0, 3), (4, 7), (1, 3))]
    spare = [pieces[p][entry, sensors : sensors + 2] for p, entry in wanted + [(5, 0)]]
    pieces, spare = lax.optimization_barrier((pieces, spare))
    spare = [v[0].astype(F32) + v[1].astype(F32) for v in spare]

    def pick(pair, other_pair, wrapped, first, wraps, ends):
        wrapped = jnp.where(ends, 0.0, wrapped)
        return jnp.where(first, pair, jnp.where(wraps, wrapped, other_pair))

    before = jnp.where(
        yh == 1,
        pick(spare[0], spare[1], spare[3], z % 2 == 1, z == 0, x == 0),
        pick(spare[5], spare[6], spare[8], z % 2 == 1, z == 0, x == 0),
    )
    after = jnp.where(
        yh == 0,
        pick(spare[0], spare[2], spare[4], z % 2 == 0, z == 7, x == 3),
        pick(spare[5], spare[7], spare[9], z % 2 == 0, z == 7, x == 3),
    )
    other = spare[10]
    coeff = jnp.concatenate(
        [
            before[-GY:],
            jnp.where(yh == 0, stiffness, other),
            jnp.where(yh == 0, other, stiffness),
            after[:GY],
        ]
    ).reshape(6, GY)

    keep, give = adjoint(pieces, forward_table(steps), inverse_table(steps_f), spectra)

    chain = [(i, i + 1) for i in range(31)]
    back = [(i + 1, i) for i in range(31)]

    field = keep + flip(give, "core").astype(F32)
    here = field[0] + flip(field[1].astype(BF), "yl").astype(F32)
    there = flip(field[2].astype(BF), "yh").astype(F32) + flip(
        field[3].astype(BF), "yh", "yl"
    ).astype(F32)
    here, there = here.reshape(2, GY, 8, NCOL), there.reshape(2, GY, 8, NCOL)
    grid = jnp.where(yh == 0, jnp.concatenate([here, there]), jnp.concatenate([there, here]))
    low = lax.ppermute(grid[-2:].astype(BF), ("x", "z"), chain)
    high = lax.ppermute(grid[:2].astype(BF), ("x", "z"), back)
    grid = jnp.concatenate([low.astype(F32), grid, high.astype(F32)])
    for sweep in range(2):
        inner = grid[1:-1]
        sides = jnp.pad(inner, ((0, 0), (1, 1), (0, 0), (0, 0)))
        beside = grid[:-2] + grid[2:] + sides[:, :-2] + sides[:, 2:]
        rows = coeff if sweep == 0 else coeff[1:-1]
        grid = inner + rows[:, :, None, None] * (beside - 4.0 * inner)
    grid = grid.astype(BF).reshape(2, PTS, 8, NCOL)
    here = jnp.where(yh == 0, grid[0], grid[1])
    there = jnp.where(yh == 0, grid[1], grid[0])
    mine = [here, flip(here, "yl"), flip(there, "yh"), flip(there, "yh", "yl")]
    other = flip(jnp.stack(mine), "core")

    outs = forward_map(mine, other, forward_table(steps_f), inverse_table(steps), spectra)
    near, back_across = outs[:5], outs[5:]

    def far_first(parts):
        low, high = from_x(parts[2], -1).astype(F32), from_x(parts[3], 1).astype(F32)
        up = jnp.concatenate([parts[1][:4] + low, parts[1][4:]]).astype(BF)
        down = jnp.concatenate([parts[4][:4], parts[4][4:] + high]).astype(BF)
        return up, down

    def gather_up(parts, up, down):
        return parts[0] + from_x(up, -1).astype(F32) + from_x(down, 1).astype(F32)

    across = gather_up(back_across, *far_first(back_across)).astype(BF)
    up, down = far_first(near)
    total = gather_up(near, up, down) + flip(across, "yh").astype(F32)
    pair = total[:2]
    parts = [from_z(total[2 * d : 2 * d + 2].astype(BF), -2 * d) for d in (1, 2, 3)]
    for part in parts:
        pair = pair + part.astype(F32)
    last = lax.ppermute(pair[1:], "z", [(i, i ^ 1) for i in range(8)])
    return (pair[:1] + last)[:, :sensors]


def solution(mesh):
    fine = Mesh(mesh.devices.reshape(4, 8, 2, 2, 2), ("x", "z", "yh", "yl", "core"))
    param, sensor = ("x", "z", "yh"), ("yl", "core")
    return jax.shard_map(
        shards,
        mesh=fine,
        in_specs=(P(param, sensor, None), P(None, None, sensor, param), P(param)),
        out_specs=P(param, sensor, None),
        check_vma=False,
    )
```

```python
import math

import jax
import jax.numpy as jnp
from jax import lax
from jax.experimental import pallas as pl
from jax.experimental.pallas import tpu as pltpu
from jax.sharding import Mesh, PartitionSpec as P

STEPS = 64
NB = STEPS + 1
GY = 64
NCOL = 128
BF = jnp.bfloat16
F32 = jnp.float32


ROWS = 152
FREQ = 128
IMAG = NB - 1
PTS = 128
BY_SENSOR = 153
BY_BIN = 129
BY_POINT = 129
ROW_GROUP = 76
POINT_GROUP = 64
BINS = 63
PIECE_STEPS = (8, 8, 4, 4, 8) * 2
PIECES = len(PIECE_STEPS)


def bins_of(shape, axis):
    row = lax.broadcasted_iota(jnp.int32, shape, axis)
    return row, jnp.where(row < NB, row, row - IMAG)


def forward_table(steps):
    row, bins = bins_of((FREQ, steps.shape[0]), 0)
    angle = (bins * steps[None, :] % (2 * STEPS)).astype(F32) * (2.0 * math.pi / (2 * STEPS))
    return jnp.where(row < NB, jnp.cos(angle), -jnp.sin(angle)) * (1.0 / math.sqrt(STEPS))


def inverse_table(steps):
    row, bins = bins_of((steps.shape[0], FREQ), 1)
    angle = (bins * steps[:, None] % (2 * STEPS)).astype(F32) * (2.0 * math.pi / (2 * STEPS))
    value = jnp.where(row < NB, jnp.cos(angle), -jnp.sin(angle)) * (1.0 / math.sqrt(STEPS))
    return value * jnp.where((bins == 0) | (bins == STEPS), 1.0, 2.0)


def rows_at(index, stride, count):
    return pl.ds(index * stride, count)


def halves(value):
    high = value.astype(BF)
    return high, (value - high.astype(F32)).astype(BF)


def dot(a, b):
    return jnp.dot(a, b, preferred_element_type=F32)


def adjoint_kernel(*refs):
    pieces = refs[:PIECES]
    fwd_ref, inv_ref, spec_ref, keep_ref, give_ref = refs[PIECES : PIECES + 5]
    adj_ref, data_ref, spec, sem = refs[PIECES + 5 :]
    time_ref = adj_ref
    copy = pltpu.make_async_copy(spec_ref, spec, sem)
    copy.start()
    i = 0
    for ref in pieces:
        for j in range(ref.shape[0]):
            time_ref[pl.ds(i * BY_SENSOR, ROWS), :] = ref[j].astype(F32)
            i += 1
    high, low = halves(fwd_ref[...])
    fwd = jnp.concatenate([high, low], axis=1)

    def to_bins(i, c):
        s0 = i * ROW_GROUP
        values = [time_ref[pl.ds(s0 + j, STEPS, stride=BY_SENSOR), :].astype(BF) for j in range(ROW_GROUP)]
        block = jnp.concatenate(values, axis=1)
        result = dot(fwd, jnp.concatenate([block, block], axis=0))
        for j in range(ROW_GROUP):
            data_ref[pl.ds(s0 + j, FREQ, stride=BY_SENSOR), :] = result[:, j * NCOL : (j + 1) * NCOL]
        return c

    lax.fori_loop(0, ROWS // ROW_GROUP, to_bins, 0)
    copy.wait()
    sensors = spec.shape[2]

    dims = (((0,), (0,)), ((), ()))
    for k in (0, STEPS):
        real = data_ref[rows_at(k, BY_SENSOR, ROWS), :][:sensors].astype(BF)
        result = lax.dot_general(spec[0, k], real, dims, preferred_element_type=F32)
        adj_ref[pl.ds(k, PTS, stride=BY_BIN), :] = result

    def one_bin(k):
        real = data_ref[rows_at(k, BY_SENSOR, ROWS), :][:sensors].astype(BF)
        imag = data_ref[rows_at(k + IMAG, BY_SENSOR, ROWS), :][:sensors].astype(BF)
        first = jnp.concatenate([real, imag], axis=1)
        second = jnp.concatenate([imag, -real], axis=1)
        result = lax.dot_general(
            spec[0, k], first, dims, preferred_element_type=F32
        ) + lax.dot_general(spec[1, k], second, dims, preferred_element_type=F32)
        adj_ref[pl.ds(k, PTS, stride=BY_BIN), :] = result[:, :NCOL]
        adj_ref[pl.ds(k + IMAG, PTS, stride=BY_BIN), :] = result[:, NCOL:]

    def some_bins(i, c):
        for j in range(BINS):
            one_bin(1 + i * BINS + j)
        return c

    lax.fori_loop(0, (STEPS - 1) // BINS, some_bins, 0)
    high, low = halves(inv_ref[...])
    inv = jnp.concatenate([high, low], axis=1)

    def to_steps(i, c):
        values = [
            adj_ref[rows_at(i * POINT_GROUP + j, BY_BIN, FREQ), :] for j in range(POINT_GROUP)
        ]
        whole = jnp.concatenate(values, axis=1).astype(BF)
        result = dot(inv, jnp.concatenate([whole, whole], axis=0))
        for j in range(POINT_GROUP):
            block = result[:, j * NCOL : (j + 1) * NCOL]
            for p in range(4):
                keep_ref[p, i * POINT_GROUP + j] = block[8 * p : 8 * p + 8]
                give_ref[p, i * POINT_GROUP + j] = block[32 + 8 * p : 40 + 8 * p].astype(BF)
        return c

    lax.fori_loop(0, PTS // POINT_GROUP, to_steps, 0)


def adjoint(pieces, fwd, inv, spectra):
    vmem = pl.BlockSpec(memory_space=pltpu.VMEM)
    return pl.pallas_call(
        adjoint_kernel,
        in_specs=[vmem] * (PIECES + 2) + [pl.BlockSpec(memory_space=pl.ANY)],
        out_specs=[vmem, vmem],
        out_shape=[
            jax.ShapeDtypeStruct((4, PTS, 8, NCOL), F32),
            jax.ShapeDtypeStruct((4, PTS, 8, NCOL), BF),
        ],
        scratch_shapes=[
            pltpu.VMEM((PTS * BY_BIN, NCOL), F32),
            pltpu.VMEM((FREQ * BY_SENSOR, NCOL), F32),
            pltpu.VMEM(spectra.shape, BF),
            pltpu.SemaphoreType.DMA,
        ],
        compiler_params=pltpu.CompilerParams(vmem_limit_bytes=27 << 20),
        name="adjoint",
    )(*pieces, fwd, inv, spectra)


def forward_kernel(*refs):
    model_in, (fwd_ref, inv_ref, spec_ref) = refs[:5], refs[5:8]
    outs, (model_ref, res_ref, spec, sem) = refs[8 : 8 + PIECES], refs[8 + PIECES :]
    copy = pltpu.make_async_copy(spec_ref, spec, sem)
    copy.start()
    high, low = halves(fwd_ref[...])
    fwd = jnp.concatenate([high, low], axis=1)

    def to_bins(i, c):
        values = [
            jnp.concatenate(
                [ref[i * POINT_GROUP + j].astype(F32) for ref in model_in[:4]]
                + [model_in[4][p, i * POINT_GROUP + j].astype(F32) for p in range(4)],
                axis=0,
            ).astype(BF)
            for j in range(POINT_GROUP)
        ]
        block = jnp.concatenate(values, axis=1)
        result = dot(fwd, jnp.concatenate([block, block], axis=0))
        for j in range(POINT_GROUP):
            model_ref[pl.ds(i * POINT_GROUP + j, FREQ, stride=BY_POINT), :] = result[:, j * NCOL : (j + 1) * NCOL]
        return c

    lax.fori_loop(0, PTS // POINT_GROUP, to_bins, 0)
    copy.wait()
    sensors = spec.shape[2]
    pad = jnp.zeros((ROWS - sensors, 2 * NCOL), F32)
    for k in (0, STEPS):
        real = model_ref[rows_at(k, BY_POINT, PTS), :].astype(BF)
        result = jnp.concatenate([dot(spec[0, k], real), pad[:, :NCOL]], axis=0)
        res_ref[pl.ds(k, ROWS, stride=BY_BIN), :] = result

    def one_bin(k):
        real = model_ref[rows_at(k, BY_POINT, PTS), :].astype(BF)
        imag = model_ref[rows_at(k + IMAG, BY_POINT, PTS), :].astype(BF)
        result = dot(spec[0, k], jnp.concatenate([real, imag], axis=1)) + dot(
            spec[1, k], jnp.concatenate([-imag, real], axis=1)
        )
        result = jnp.concatenate([result, pad], axis=0)
        res_ref[pl.ds(k, ROWS, stride=BY_BIN), :] = result[:, :NCOL]
        res_ref[pl.ds(k + IMAG, ROWS, stride=BY_BIN), :] = result[:, NCOL:]

    def some_bins(i, c):
        for j in range(BINS):
            one_bin(1 + i * BINS + j)
        return c

    lax.fori_loop(0, (STEPS - 1) // BINS, some_bins, 0)

    high, low = halves(inv_ref[...])
    inv = jnp.concatenate([high, low], axis=1)

    def to_steps(i, c):
        values = [
            res_ref[rows_at(i * ROW_GROUP + j, BY_BIN, FREQ), :] for j in range(ROW_GROUP)
        ]
        whole = jnp.concatenate(values, axis=1).astype(BF)
        result = dot(inv, jnp.concatenate([whole, whole], axis=0))
        for j in range(ROW_GROUP):
            model_ref[pl.ds(i * ROW_GROUP + j, STEPS, stride=BY_SENSOR), :] = result[:, j * NCOL : (j + 1) * NCOL]
        return c

    lax.fori_loop(0, ROWS // ROW_GROUP, to_steps, 0)
    i = 0
    for ref in outs:
        for j in range(ref.shape[0]):
            ref[j] = model_ref[pl.ds(i * BY_SENSOR, ROWS), :].astype(ref.dtype)
            i += 1


def forward_map(mine, other, fwd, inv, spectra):
    vmem = pl.BlockSpec(memory_space=pltpu.VMEM)
    return pl.pallas_call(
        forward_kernel,
        in_specs=[vmem] * 7 + [pl.BlockSpec(memory_space=pl.ANY)],
        out_specs=[vmem] * PIECES,
        out_shape=[
            jax.ShapeDtypeStruct((count, ROWS, NCOL), BF if count == 4 else F32)
            for count in PIECE_STEPS
        ],
        scratch_shapes=[
            pltpu.VMEM((FREQ * BY_POINT, NCOL), F32),
            pltpu.VMEM((ROWS * BY_BIN, NCOL), F32),
            pltpu.VMEM(spectra.shape, BF),
            pltpu.SemaphoreType.DMA,
        ],
        compiler_params=pltpu.CompilerParams(vmem_limit_bytes=27 << 20),
        name="forward_map",
    )(*mine, other, fwd, inv, spectra)


def from_x(v, d):
    return lax.ppermute(v, "x", [((i + d) % 4, i) for i in range(4)])


def flip(v, *axes):
    size = 2 ** len(axes)
    return lax.ppermute(v, axes, [(i, size - 1 - i) for i in range(size)])


def shards(readings, spectra, stiffness):
    x, z, yh = lax.axis_index("x"), lax.axis_index("z"), lax.axis_index("yh")
    yl, core = lax.axis_index("yl"), lax.axis_index("core")
    sensors = readings.shape[1]
    i = jnp.arange(STEPS, dtype=jnp.int32)
    steps = (
        (x + i // 8) % 4 * 16 + i % 8 * 2 + (yh ^ (i // 32))
    )
    steps_f = ((core ^ (i // 32)) * 4 + (yh ^ (i // 16 % 2)) * 2 + (yl ^ (i // 8 % 2))) * 8 + i % 8

    high = lax.reduce_precision(stiffness, 8, 7)
    column = jnp.concatenate(
        [readings, high.astype(BF)[None, None], (stiffness - high).astype(BF)[None, None]], axis=1
    )
    column = lax.all_to_all(jnp.broadcast_to(column, (8,) + column.shape[1:]), "z", 0, 0, tiled=True)
    up, down, across = from_x(column, 1), from_x(column, -1), flip(column, "yh")
    far = [from_x(up[:4], 1), from_x(down[4:], -1)]
    pieces = [column, up] + far + [down]
    up, down = from_x(across, 1), from_x(across, -1)
    far = [from_x(up[:4], 1), from_x(down[4:], -1)]
    pieces += [across, up] + far + [down]

    def spare_rows(piece, place):
        return lax.dynamic_slice(piece, (place, sensors, 0), (1, 2, NCOL))[0]

    wanted = [(q + p, at % 8) for q in (0, 5) for p, at in ((0, z - 1), (0, z + 1), (4, 7), (1, 0))]
    spare = [spare_rows(pieces[p], at) for p, at in wanted + [(5, z)]]
    pieces, spare = lax.optimization_barrier((pieces, spare))
    spare = [v[0].astype(F32) + v[1].astype(F32) for v in spare]

    def pick(inside, wrapped, wraps, ends):
        return jnp.where(wraps, jnp.where(ends, 0.0, wrapped), inside)

    before = jnp.where(
        yh == 1,
        pick(spare[0], spare[2], z == 0, x == 0),
        pick(spare[4], spare[6], z == 0, x == 0),
    )
    after = jnp.where(
        yh == 0,
        pick(spare[1], spare[3], z == 7, x == 3),
        pick(spare[5], spare[7], z == 7, x == 3),
    )
    other = spare[8]
    coeff = jnp.concatenate(
        [
            before[-GY:],
            jnp.where(yh == 0, stiffness, other),
            jnp.where(yh == 0, other, stiffness),
            after[:GY],
        ]
    ).reshape(6, GY)

    keep, give = adjoint(pieces, forward_table(steps), inverse_table(steps_f), spectra)

    on = [(b, b + 1) for b in range(31)]
    outward = [(2 * d, 2 * b) for b, d in on] + [(2 * b + 1, 2 * d + 1) for b, d in on]
    inward = [(2 * b, 2 * d) for b, d in on] + [(2 * d + 1, 2 * b + 1) for b, d in on]

    field = keep + flip(give, "core").astype(F32)
    here = field[0] + flip(field[1].astype(BF), "yl").astype(F32)
    there = flip(field[2].astype(BF), "yh").astype(F32) + flip(
        field[3].astype(BF), "yh", "yl"
    ).astype(F32)
    here, there = here.reshape(2, GY, 8, NCOL), there.reshape(2, GY, 8, NCOL)
    first = lax.ppermute(here.astype(BF), ("x", "z", "yh"), outward).astype(F32)
    second = lax.ppermute(there.astype(BF), ("x", "z", "yh"), inward).astype(F32)
    grid = jnp.where(
        yh == 0,
        jnp.concatenate([second, here, there, first]),
        jnp.concatenate([first, there, here, second]),
    )
    for sweep in range(2):
        inner = grid[1:-1]
        sides = jnp.pad(inner, ((0, 0), (1, 1), (0, 0), (0, 0)))
        beside = grid[:-2] + grid[2:] + sides[:, :-2] + sides[:, 2:]
        rows = coeff if sweep == 0 else coeff[1:-1]
        grid = inner + rows[:, :, None, None] * (beside - 4.0 * inner)
    grid = grid.astype(BF).reshape(2, PTS, 8, NCOL)
    here = jnp.where(yh == 0, grid[0], grid[1])
    there = jnp.where(yh == 0, grid[1], grid[0])
    mine = [here, flip(here, "yl"), flip(there, "yh"), flip(there, "yh", "yl")]
    other = flip(jnp.stack(mine), "core")

    outs = forward_map(mine, other, forward_table(steps_f), inverse_table(steps), spectra)
    near, back_across = outs[:5], outs[5:]

    def far_first(parts):
        low, high = from_x(parts[2], -1).astype(F32), from_x(parts[3], 1).astype(F32)
        up = jnp.concatenate([parts[1][:4] + low, parts[1][4:]]).astype(BF)
        down = jnp.concatenate([parts[4][:4], parts[4][4:] + high]).astype(BF)
        return up, down

    def gather_up(parts, up, down):
        return parts[0] + from_x(up, -1).astype(F32) + from_x(down, 1).astype(F32)

    across = gather_up(back_across, *far_first(back_across)).astype(BF)
    up, down = far_first(near)
    total = gather_up(near, up, down) + flip(across, "yh").astype(F32)
    total = lax.all_to_all(total.astype(BF), "z", 0, 0, tiled=True).astype(F32)
    return jnp.sum(total, axis=0, keepdims=True)[:, :sensors]


def solution(mesh):
    fine = Mesh(mesh.devices.reshape(4, 8, 2, 2, 2), ("x", "z", "yh", "yl", "core"))
    param, sensor = ("x", "z", "yh"), ("yl", "core")
    return jax.shard_map(
        shards,
        mesh=fine,
        in_specs=(P(param, sensor, None), P(None, None, sensor, param), P(param)),
        out_specs=P(param, sensor, None),
        check_vma=False,
    )
```

```python
import math

import jax
import jax.numpy as jnp
from jax import lax
from jax.experimental import pallas as pl
from jax.experimental.pallas import tpu as pltpu
from jax.sharding import Mesh, PartitionSpec as P

STEPS = 64
NB = STEPS + 1
GY = 64
NCOL = 128
BF = jnp.bfloat16
F32 = jnp.float32


ROWS = 152
FREQ = 128
IMAG = NB - 1
PTS = 128
BY_SENSOR = 153
BY_BIN = 129
BY_POINT = 129
ROW_GROUP = 76
POINT_GROUP = 64
BINS = 63
PIECE_STEPS = (8, 8, 4, 4, 8) * 2
PIECES = len(PIECE_STEPS)


def bins_of(shape, axis):
    row = lax.broadcasted_iota(jnp.int32, shape, axis)
    return row, jnp.where(row < NB, row, row - IMAG)


def forward_table(steps):
    row, bins = bins_of((FREQ, steps.shape[0]), 0)
    angle = (bins * steps[None, :] % (2 * STEPS)).astype(F32) * (2.0 * math.pi / (2 * STEPS))
    return jnp.where(row < NB, jnp.cos(angle), -jnp.sin(angle)) * (1.0 / math.sqrt(STEPS))


def inverse_table(steps):
    row, bins = bins_of((steps.shape[0], FREQ), 1)
    angle = (bins * steps[:, None] % (2 * STEPS)).astype(F32) * (2.0 * math.pi / (2 * STEPS))
    value = jnp.where(row < NB, jnp.cos(angle), -jnp.sin(angle)) * (1.0 / math.sqrt(STEPS))
    return value * jnp.where((bins == 0) | (bins == STEPS), 1.0, 2.0)


def rows_at(index, stride, count):
    return pl.ds(index * stride, count)


def halves(value):
    high = value.astype(BF)
    return high, (value - high.astype(F32)).astype(BF)


def dot(a, b):
    return jnp.dot(a, b, preferred_element_type=F32)


def adjoint_kernel(*refs):
    pieces = refs[:-9]
    fwd_ref, inv_ref, spec_ref, keep_ref, give_ref = refs[-9:-4]
    adj_ref, data_ref, spec, sem = refs[-4:]
    time_ref = adj_ref
    copy = pltpu.make_async_copy(spec_ref, spec, sem)
    copy.start()
    i = 0
    for ref in pieces:
        for j in range(ref.shape[0]):
            time_ref[pl.ds(i * BY_SENSOR, ROWS), :] = ref[j].astype(F32)
            i += 1
    high, low = halves(fwd_ref[...])
    fwd = jnp.concatenate([high, low], axis=1)

    def to_bins(i, c):
        s0 = i * ROW_GROUP
        values = [time_ref[pl.ds(s0 + j, STEPS, stride=BY_SENSOR), :].astype(BF) for j in range(ROW_GROUP)]
        block = jnp.concatenate(values, axis=1)
        result = dot(fwd, jnp.concatenate([block, block], axis=0))
        for j in range(ROW_GROUP):
            data_ref[pl.ds(s0 + j, FREQ, stride=BY_SENSOR), :] = result[:, j * NCOL : (j + 1) * NCOL]
        return c

    lax.fori_loop(0, ROWS // ROW_GROUP, to_bins, 0)
    copy.wait()
    sensors = spec.shape[2]

    dims = (((0,), (0,)), ((), ()))
    for k in (0, STEPS):
        real = data_ref[rows_at(k, BY_SENSOR, ROWS), :][:sensors].astype(BF)
        result = lax.dot_general(spec[0, k], real, dims, preferred_element_type=F32)
        adj_ref[pl.ds(k, PTS, stride=BY_BIN), :] = result

    def one_bin(k):
        real = data_ref[rows_at(k, BY_SENSOR, ROWS), :][:sensors].astype(BF)
        imag = data_ref[rows_at(k + IMAG, BY_SENSOR, ROWS), :][:sensors].astype(BF)
        first = jnp.concatenate([real, imag], axis=1)
        second = jnp.concatenate([imag, -real], axis=1)
        result = lax.dot_general(
            spec[0, k], first, dims, preferred_element_type=F32
        ) + lax.dot_general(spec[1, k], second, dims, preferred_element_type=F32)
        adj_ref[pl.ds(k, PTS, stride=BY_BIN), :] = result[:, :NCOL]
        adj_ref[pl.ds(k + IMAG, PTS, stride=BY_BIN), :] = result[:, NCOL:]

    def some_bins(i, c):
        for j in range(BINS):
            one_bin(1 + i * BINS + j)
        return c

    lax.fori_loop(0, (STEPS - 1) // BINS, some_bins, 0)
    high, low = halves(inv_ref[...])
    inv = jnp.concatenate([high, low], axis=1)

    def to_steps(i, c):
        values = [
            adj_ref[rows_at(i * POINT_GROUP + j, BY_BIN, FREQ), :] for j in range(POINT_GROUP)
        ]
        whole = jnp.concatenate(values, axis=1).astype(BF)
        result = dot(inv, jnp.concatenate([whole, whole], axis=0))
        for j in range(POINT_GROUP):
            block = result[:, j * NCOL : (j + 1) * NCOL]
            for p in range(4):
                keep_ref[p, i * POINT_GROUP + j] = block[8 * p : 8 * p + 8]
                give_ref[p, i * POINT_GROUP + j] = block[32 + 8 * p : 40 + 8 * p].astype(BF)
        return c

    lax.fori_loop(0, PTS // POINT_GROUP, to_steps, 0)


def adjoint(pieces, fwd, inv, spectra):
    vmem = pl.BlockSpec(memory_space=pltpu.VMEM)
    return pl.pallas_call(
        adjoint_kernel,
        in_specs=[vmem] * (len(pieces) + 2) + [pl.BlockSpec(memory_space=pltpu.HBM)],
        out_specs=[vmem, vmem],
        out_shape=[
            jax.ShapeDtypeStruct((4, PTS, 8, NCOL), F32),
            jax.ShapeDtypeStruct((4, PTS, 8, NCOL), BF),
        ],
        scratch_shapes=[
            pltpu.VMEM((PTS * BY_BIN, NCOL), F32),
            pltpu.VMEM((FREQ * BY_SENSOR, NCOL), F32),
            pltpu.VMEM(spectra.shape, BF),
            pltpu.SemaphoreType.DMA,
        ],
        compiler_params=pltpu.CompilerParams(vmem_limit_bytes=27 << 20),
        name="adjoint",
    )(*pieces, fwd, inv, spectra)


def forward_kernel(*refs):
    model_in, (fwd_ref, inv_ref, spec_ref) = refs[:8], refs[8:11]
    outs, (model_ref, res_ref, spec, sem) = refs[11 : 11 + PIECES], refs[11 + PIECES :]
    copy = pltpu.make_async_copy(spec_ref, spec, sem)
    copy.start()
    high, low = halves(fwd_ref[...])
    fwd = jnp.concatenate([high, low], axis=1)

    def to_bins(i, c):
        values = [
            jnp.concatenate(
                [ref[i * POINT_GROUP + j].astype(F32) for ref in model_in],
                axis=0,
            ).astype(BF)
            for j in range(POINT_GROUP)
        ]
        block = jnp.concatenate(values, axis=1)
        result = dot(fwd, jnp.concatenate([block, block], axis=0))
        for j in range(POINT_GROUP):
            model_ref[pl.ds(i * POINT_GROUP + j, FREQ, stride=BY_POINT), :] = result[:, j * NCOL : (j + 1) * NCOL]
        return c

    lax.fori_loop(0, PTS // POINT_GROUP, to_bins, 0)
    copy.wait()
    sensors = spec.shape[2]
    pad = jnp.zeros((ROWS - sensors, 2 * NCOL), F32)
    for k in (0, STEPS):
        real = model_ref[rows_at(k, BY_POINT, PTS), :].astype(BF)
        result = jnp.concatenate([dot(spec[0, k], real), pad[:, :NCOL]], axis=0)
        res_ref[pl.ds(k, ROWS, stride=BY_BIN), :] = result

    def one_bin(k):
        real = model_ref[rows_at(k, BY_POINT, PTS), :].astype(BF)
        imag = model_ref[rows_at(k + IMAG, BY_POINT, PTS), :].astype(BF)
        result = dot(spec[0, k], jnp.concatenate([real, imag], axis=1)) + dot(
            spec[1, k], jnp.concatenate([-imag, real], axis=1)
        )
        result = jnp.concatenate([result, pad], axis=0)
        res_ref[pl.ds(k, ROWS, stride=BY_BIN), :] = result[:, :NCOL]
        res_ref[pl.ds(k + IMAG, ROWS, stride=BY_BIN), :] = result[:, NCOL:]

    def some_bins(i, c):
        for j in range(BINS):
            one_bin(1 + i * BINS + j)
        return c

    lax.fori_loop(0, (STEPS - 1) // BINS, some_bins, 0)

    high, low = halves(inv_ref[...])
    inv = jnp.concatenate([high, low], axis=1)

    def to_steps(i, c):
        values = [
            res_ref[rows_at(i * ROW_GROUP + j, BY_BIN, FREQ), :] for j in range(ROW_GROUP)
        ]
        whole = jnp.concatenate(values, axis=1).astype(BF)
        result = dot(inv, jnp.concatenate([whole, whole], axis=0))
        for j in range(ROW_GROUP):
            model_ref[pl.ds(i * ROW_GROUP + j, STEPS, stride=BY_SENSOR), :] = result[:, j * NCOL : (j + 1) * NCOL]
        return c

    lax.fori_loop(0, ROWS // ROW_GROUP, to_steps, 0)
    i = 0
    for ref in outs:
        for j in range(ref.shape[0]):
            ref[j] = model_ref[pl.ds(i * BY_SENSOR, ROWS), :].astype(ref.dtype)
            i += 1


def forward_map(mine, other, fwd, inv, spectra):
    vmem = pl.BlockSpec(memory_space=pltpu.VMEM)
    return pl.pallas_call(
        forward_kernel,
        in_specs=[vmem] * 10 + [pl.BlockSpec(memory_space=pltpu.HBM)],
        out_specs=[vmem] * PIECES,
        out_shape=[
            jax.ShapeDtypeStruct((count, ROWS, NCOL), BF if count == 4 else F32)
            for count in PIECE_STEPS
        ],
        scratch_shapes=[
            pltpu.VMEM((FREQ * BY_POINT, NCOL), F32),
            pltpu.VMEM((ROWS * BY_BIN, NCOL), F32),
            pltpu.VMEM(spectra.shape, BF),
            pltpu.SemaphoreType.DMA,
        ],
        compiler_params=pltpu.CompilerParams(vmem_limit_bytes=27 << 20),
        name="forward_map",
    )(*mine, *other, fwd, inv, spectra)


def from_x(v, d):
    return lax.ppermute(v, "x", [((i + d) % 4, i) for i in range(4)])


def flip(v, *axes):
    size = 2 ** len(axes)
    return lax.ppermute(v, axes, [(i, size - 1 - i) for i in range(size)])


def shards(readings, spectra, stiffness):
    x, z, yh = lax.axis_index("x"), lax.axis_index("z"), lax.axis_index("yh")
    yl, core = lax.axis_index("yl"), lax.axis_index("core")
    sensors = readings.shape[1]
    i = jnp.arange(STEPS, dtype=jnp.int32)
    steps = (
        (x + i // 8) % 4 * 16 + i % 8 * 2 + (yh ^ (i // 32))
    )
    place = jnp.where(i < 48, i // 8, (9 - i // 8) % 4 + 4)
    gathered = (
        (x + place) % 4 * 16 + i % 8 * 2 + (yh ^ (i // 32))
    )
    steps_f = ((core ^ (i // 32)) * 4 + (yh ^ (i // 16 % 2)) * 2 + (yl ^ (i // 8 % 2))) * 8 + i % 8

    high = lax.reduce_precision(stiffness, 8, 7)
    column = jnp.concatenate(
        [readings, high.astype(BF)[None, None], (stiffness - high).astype(BF)[None, None]], axis=1
    )
    column = lax.all_to_all(jnp.broadcast_to(column, (8,) + column.shape[1:]), "z", 0, 0, tiled=True)
    up, down, across = from_x(column, 1), from_x(column, -1), flip(column, "yh")
    far = [from_x(up[:4], 1), from_x(down[4:], -1)]
    pieces = [column, up] + far + [down]
    beside = flip(jnp.concatenate([up[4:], down[:4]]), "yh")
    up, down = from_x(across[:4], 1), from_x(across[4:], -1)
    pieces += [across, up, beside, down, from_x(up, 1), from_x(down, -1)]

    def spare_rows(piece, place):
        return lax.dynamic_slice(piece, (place, sensors, 0), (1, 2, NCOL))[0]

    wanted = [
        (p, at % 8)
        for own, down, last, up in ((0, 4, 7, 1), (5, 8, 3, 6))
        for p, at in ((own, z - 1), (own, z + 1), (down, last), (up, 0))
    ]
    spare = [spare_rows(pieces[p], at) for p, at in wanted + [(5, z)]]
    pieces, spare = lax.optimization_barrier((pieces, spare))
    spare = [v[0].astype(F32) + v[1].astype(F32) for v in spare]

    def pick(inside, wrapped, wraps, ends):
        return jnp.where(wraps, jnp.where(ends, 0.0, wrapped), inside)

    before = jnp.where(
        yh == 1,
        pick(spare[0], spare[2], z == 0, x == 0),
        pick(spare[4], spare[6], z == 0, x == 0),
    )
    after = jnp.where(
        yh == 0,
        pick(spare[1], spare[3], z == 7, x == 3),
        pick(spare[5], spare[7], z == 7, x == 3),
    )
    other = spare[8]
    coeff = jnp.concatenate(
        [
            before[-GY:],
            jnp.where(yh == 0, stiffness, other),
            jnp.where(yh == 0, other, stiffness),
            after[:GY],
        ]
    ).reshape(6, GY)

    spectra = pltpu.with_memory_space_constraint(spectra, pltpu.HBM)
    keep, give = adjoint(pieces, forward_table(gathered), inverse_table(steps_f), spectra)

    on = [(b, b + 1) for b in range(31)]
    outward = [(2 * d, 2 * b) for b, d in on] + [(2 * b + 1, 2 * d + 1) for b, d in on]
    inward = [(2 * b, 2 * d) for b, d in on] + [(2 * d + 1, 2 * b + 1) for b, d in on]

    field = keep + flip(give, "core").astype(F32)
    here = field[0] + flip(field[1].astype(BF), "yl").astype(F32)
    there = flip(field[2].astype(BF), "yh").astype(F32) + flip(
        field[3].astype(BF), "yh", "yl"
    ).astype(F32)
    here, there = here.reshape(2, GY, 8, NCOL), there.reshape(2, GY, 8, NCOL)
    first = lax.ppermute(here.astype(BF), ("x", "z", "yh"), outward).astype(F32)
    second = lax.ppermute(there.astype(BF), ("x", "z", "yh"), inward).astype(F32)
    grid = jnp.where(
        yh == 0,
        jnp.concatenate([second, here, there, first]),
        jnp.concatenate([first, there, here, second]),
    )
    for sweep in range(2):
        inner = grid[1:-1]
        sides = jnp.pad(inner, ((0, 0), (1, 1), (0, 0), (0, 0)))
        beside = grid[:-2] + grid[2:] + sides[:, :-2] + sides[:, 2:]
        rows = coeff if sweep == 0 else coeff[1:-1]
        grid = inner + rows[:, :, None, None] * (beside - 4.0 * inner)
    grid = grid.astype(BF).reshape(2, PTS, 8, NCOL)
    here = jnp.where(yh == 0, grid[0], grid[1])
    there = jnp.where(yh == 0, grid[1], grid[0])
    mine = [here, flip(here, "yl"), flip(there, "yh"), flip(there, "yh", "yl")]
    other = [flip(part, "core") for part in mine]

    outs = forward_map(mine, other, forward_table(steps_f), inverse_table(steps), spectra)
    near, back_across = outs[:5], outs[5:]

    def far_first(parts):
        low, high = from_x(parts[2], -1).astype(F32), from_x(parts[3], 1).astype(F32)
        up = jnp.concatenate([parts[1][:4] + low, parts[1][4:]]).astype(BF)
        down = jnp.concatenate([parts[4][:4], parts[4][4:] + high]).astype(BF)
        return up, down

    def gather_up(parts, up, down):
        return parts[0] + from_x(up, -1).astype(F32) + from_x(down, 1).astype(F32)

    across = gather_up(back_across, *far_first(back_across)).astype(BF)
    up, down = far_first(near)
    total = gather_up(near, up, down) + flip(across, "yh").astype(F32)
    total = lax.all_to_all(total.astype(BF), "z", 0, 0, tiled=True).astype(F32)
    return jnp.sum(total, axis=0, keepdims=True)[:, :sensors]


def solution(mesh):
    fine = Mesh(mesh.devices.reshape(4, 8, 2, 2, 2), ("x", "z", "yh", "yl", "core"))
    param, sensor = ("x", "z", "yh"), ("yl", "core")
    return jax.shard_map(
        shards,
        mesh=fine,
        in_specs=(P(param, sensor, None), P(None, None, sensor, param), P(param)),
        out_specs=P(param, sensor, None),
        check_vma=False,
    )
```

```python
import math

import jax
import jax.numpy as jnp
from jax import lax
from jax.experimental import pallas as pl
from jax.experimental.pallas import tpu as pltpu
from jax.sharding import Mesh, PartitionSpec as P

STEPS = 64
NB = STEPS + 1
GY = 64
NCOL = 128
BF = jnp.bfloat16
F32 = jnp.float32


ROWS = 152
FREQ = 128
IMAG = NB - 1
PTS = 128
BY_SENSOR = 153
BY_BIN = 129
BY_POINT = 129
ROW_GROUP = 76
POINT_GROUP = 64
BINS = 63
PIECE_STEPS = (8, 8, 4, 4, 8) * 2
PIECES = len(PIECE_STEPS)


def bins_of(shape, axis):
    row = lax.broadcasted_iota(jnp.int32, shape, axis)
    return row, jnp.where(row < NB, row, row - IMAG)


def forward_table(steps):
    row, bins = bins_of((FREQ, steps.shape[0]), 0)
    angle = (bins * steps[None, :] % (2 * STEPS)).astype(F32) * (2.0 * math.pi / (2 * STEPS))
    return jnp.where(row < NB, jnp.cos(angle), -jnp.sin(angle)) * (1.0 / math.sqrt(STEPS))


def inverse_table(steps):
    row, bins = bins_of((steps.shape[0], FREQ), 1)
    angle = (bins * steps[:, None] % (2 * STEPS)).astype(F32) * (2.0 * math.pi / (2 * STEPS))
    value = jnp.where(row < NB, jnp.cos(angle), -jnp.sin(angle)) * (1.0 / math.sqrt(STEPS))
    return value * jnp.where((bins == 0) | (bins == STEPS), 1.0, 2.0)


def rows_at(index, stride, count):
    return pl.ds(index * stride, count)


def halves(value):
    high = value.astype(BF)
    return high, (value - high.astype(F32)).astype(BF)


def dot(a, b):
    return jnp.dot(a, b, preferred_element_type=F32)


def adjoint_kernel(*refs):
    pieces = refs[:-9]
    fwd_ref, inv_ref, spec_ref, keep_ref, give_ref = refs[-9:-4]
    adj_ref, data_ref, spec, sem = refs[-4:]
    time_ref = adj_ref
    copy = pltpu.make_async_copy(spec_ref, spec, sem)
    copy.start()
    i = 0
    for ref in pieces:
        for j in range(ref.shape[0]):
            time_ref[pl.ds(i * BY_SENSOR, ROWS), :] = ref[j].astype(F32)
            i += 1
    high, low = halves(fwd_ref[...])
    fwd = jnp.concatenate([high, low], axis=1)

    def to_bins(i, c):
        s0 = i * ROW_GROUP
        values = [time_ref[pl.ds(s0 + j, STEPS, stride=BY_SENSOR), :].astype(BF) for j in range(ROW_GROUP)]
        block = jnp.concatenate(values, axis=1)
        result = dot(fwd, jnp.concatenate([block, block], axis=0))
        for j in range(ROW_GROUP):
            data_ref[pl.ds(s0 + j, FREQ, stride=BY_SENSOR), :] = result[:, j * NCOL : (j + 1) * NCOL]
        return c

    lax.fori_loop(0, ROWS // ROW_GROUP, to_bins, 0)
    copy.wait()
    sensors = spec.shape[2]

    dims = (((0,), (0,)), ((), ()))
    for k in (0, STEPS):
        real = data_ref[rows_at(k, BY_SENSOR, ROWS), :][:sensors].astype(BF)
        result = lax.dot_general(spec[0, k], real, dims, preferred_element_type=F32)
        adj_ref[pl.ds(k, PTS, stride=BY_BIN), :] = result

    def one_bin(k):
        real = data_ref[rows_at(k, BY_SENSOR, ROWS), :][:sensors].astype(BF)
        imag = data_ref[rows_at(k + IMAG, BY_SENSOR, ROWS), :][:sensors].astype(BF)
        first = jnp.concatenate([real, imag], axis=1)
        second = jnp.concatenate([imag, -real], axis=1)
        result = lax.dot_general(
            spec[0, k], first, dims, preferred_element_type=F32
        ) + lax.dot_general(spec[1, k], second, dims, preferred_element_type=F32)
        adj_ref[pl.ds(k, PTS, stride=BY_BIN), :] = result[:, :NCOL]
        adj_ref[pl.ds(k + IMAG, PTS, stride=BY_BIN), :] = result[:, NCOL:]

    def some_bins(i, c):
        for j in range(BINS):
            one_bin(1 + i * BINS + j)
        return c

    lax.fori_loop(0, (STEPS - 1) // BINS, some_bins, 0)
    high, low = halves(inv_ref[...])
    inv = jnp.concatenate([high, low], axis=1)

    def to_steps(i, c):
        values = [
            adj_ref[rows_at(i * POINT_GROUP + j, BY_BIN, FREQ), :] for j in range(POINT_GROUP)
        ]
        whole = jnp.concatenate(values, axis=1).astype(BF)
        result = dot(inv, jnp.concatenate([whole, whole], axis=0))
        for j in range(POINT_GROUP):
            block = result[:, j * NCOL : (j + 1) * NCOL]
            for p in range(4):
                keep_ref[p, i * POINT_GROUP + j] = block[8 * p : 8 * p + 8]
                give_ref[p, i * POINT_GROUP + j] = block[32 + 8 * p : 40 + 8 * p].astype(BF)
        return c

    lax.fori_loop(0, PTS // POINT_GROUP, to_steps, 0)


def adjoint(pieces, fwd, inv, spectra):
    vmem = pl.BlockSpec(memory_space=pltpu.VMEM)
    return pl.pallas_call(
        adjoint_kernel,
        in_specs=[vmem] * (len(pieces) + 2) + [pl.BlockSpec(memory_space=pltpu.HBM)],
        out_specs=[vmem, vmem],
        out_shape=[
            jax.ShapeDtypeStruct((4, PTS, 8, NCOL), F32),
            jax.ShapeDtypeStruct((4, PTS, 8, NCOL), BF),
        ],
        scratch_shapes=[
            pltpu.VMEM((PTS * BY_BIN, NCOL), F32),
            pltpu.VMEM((FREQ * BY_SENSOR, NCOL), F32),
            pltpu.VMEM(spectra.shape, BF),
            pltpu.SemaphoreType.DMA,
        ],
        compiler_params=pltpu.CompilerParams(vmem_limit_bytes=27 << 20),
        name="adjoint",
    )(*pieces, fwd, inv, spectra)


def forward_kernel(*refs):
    model_in, (fwd_ref, inv_ref, spec_ref) = refs[:8], refs[8:11]
    outs, (model_ref, res_ref, spec, sem) = refs[11 : 11 + PIECES], refs[11 + PIECES :]
    copy = pltpu.make_async_copy(spec_ref, spec, sem)
    copy.start()
    high, low = halves(fwd_ref[...])
    fwd = jnp.concatenate([high, low], axis=1)

    def to_bins(i, c):
        values = [
            jnp.concatenate(
                [ref[i * POINT_GROUP + j].astype(F32) for ref in model_in],
                axis=0,
            ).astype(BF)
            for j in range(POINT_GROUP)
        ]
        block = jnp.concatenate(values, axis=1)
        result = dot(fwd, jnp.concatenate([block, block], axis=0))
        for j in range(POINT_GROUP):
            model_ref[pl.ds(i * POINT_GROUP + j, FREQ, stride=BY_POINT), :] = result[:, j * NCOL : (j + 1) * NCOL]
        return c

    lax.fori_loop(0, PTS // POINT_GROUP, to_bins, 0)
    copy.wait()
    sensors = spec.shape[2]
    pad = jnp.zeros((ROWS - sensors, 2 * NCOL), F32)
    for k in (0, STEPS):
        real = model_ref[rows_at(k, BY_POINT, PTS), :].astype(BF)
        result = jnp.concatenate([dot(spec[0, k], real), pad[:, :NCOL]], axis=0)
        res_ref[pl.ds(k, ROWS, stride=BY_BIN), :] = result

    def one_bin(k):
        real = model_ref[rows_at(k, BY_POINT, PTS), :].astype(BF)
        imag = model_ref[rows_at(k + IMAG, BY_POINT, PTS), :].astype(BF)
        result = dot(spec[0, k], jnp.concatenate([real, imag], axis=1)) + dot(
            spec[1, k], jnp.concatenate([-imag, real], axis=1)
        )
        result = jnp.concatenate([result, pad], axis=0)
        res_ref[pl.ds(k, ROWS, stride=BY_BIN), :] = result[:, :NCOL]
        res_ref[pl.ds(k + IMAG, ROWS, stride=BY_BIN), :] = result[:, NCOL:]

    def some_bins(i, c):
        for j in range(BINS):
            one_bin(1 + i * BINS + j)
        return c

    lax.fori_loop(0, (STEPS - 1) // BINS, some_bins, 0)

    high, low = halves(inv_ref[...])
    inv = jnp.concatenate([high, low], axis=1)

    def to_steps(i, c):
        values = [
            res_ref[rows_at(i * ROW_GROUP + j, BY_BIN, FREQ), :] for j in range(ROW_GROUP)
        ]
        whole = jnp.concatenate(values, axis=1).astype(BF)
        result = dot(inv, jnp.concatenate([whole, whole], axis=0))
        for j in range(ROW_GROUP):
            model_ref[pl.ds(i * ROW_GROUP + j, STEPS, stride=BY_SENSOR), :] = result[:, j * NCOL : (j + 1) * NCOL]
        return c

    lax.fori_loop(0, ROWS // ROW_GROUP, to_steps, 0)
    i = 0
    for ref in outs:
        for j in range(ref.shape[0]):
            ref[j] = model_ref[pl.ds(i * BY_SENSOR, ROWS), :].astype(ref.dtype)
            i += 1


def forward_map(mine, other, fwd, inv, spectra):
    vmem = pl.BlockSpec(memory_space=pltpu.VMEM)
    return pl.pallas_call(
        forward_kernel,
        in_specs=[vmem] * 10 + [pl.BlockSpec(memory_space=pltpu.HBM)],
        out_specs=[vmem] * PIECES,
        out_shape=[
            jax.ShapeDtypeStruct((count, ROWS, NCOL), BF if count == 4 else F32)
            for count in PIECE_STEPS
        ],
        scratch_shapes=[
            pltpu.VMEM((FREQ * BY_POINT, NCOL), F32),
            pltpu.VMEM((ROWS * BY_BIN, NCOL), F32),
            pltpu.VMEM(spectra.shape, BF),
            pltpu.SemaphoreType.DMA,
        ],
        compiler_params=pltpu.CompilerParams(vmem_limit_bytes=27 << 20),
        name="forward_map",
    )(*mine, *other, fwd, inv, spectra)


def from_x(v, d):
    return lax.ppermute(v, "x", [((i + d) % 4, i) for i in range(4)])


def flip(v, *axes):
    size = 2 ** len(axes)
    return lax.ppermute(v, axes, [(i, size - 1 - i) for i in range(size)])


def shards(readings, spectra, stiffness):
    x, z, yh = lax.axis_index("x"), lax.axis_index("z"), lax.axis_index("yh")
    yl, core = lax.axis_index("yl"), lax.axis_index("core")
    sensors = readings.shape[1]
    i = jnp.arange(STEPS, dtype=jnp.int32)
    steps = (
        (x + i // 8) % 4 * 16 + i % 8 * 2 + (yh ^ (i // 32))
    )
    place = jnp.where(i < 48, i // 8, (9 - i // 8) % 4 + 4)
    gathered = (
        (x + place) % 4 * 16 + i % 8 * 2 + (yh ^ (i // 32))
    )
    steps_f = ((core ^ (i // 32)) * 4 + (yh ^ (i // 16 % 2)) * 2 + (yl ^ (i // 8 % 2))) * 8 + i % 8

    high = lax.reduce_precision(stiffness, 8, 7)
    column = jnp.concatenate(
        [readings, high.astype(BF)[None, None], (stiffness - high).astype(BF)[None, None]], axis=1
    )
    column = lax.all_to_all(jnp.broadcast_to(column, (8,) + column.shape[1:]), "z", 0, 0, tiled=True)
    up, down, across = from_x(column, 1), from_x(column, -1), flip(column, "yh")
    far = [from_x(up[:4], 1), from_x(down[4:], -1)]
    pieces = [column, up] + far + [down]
    beside = flip(jnp.concatenate([up[4:], down[:4]]), "yh")
    up, down = from_x(across[:4], 1), from_x(across[4:], -1)
    pieces += [across, up, beside, down, from_x(up, 1), from_x(down, -1)]

    def spare_rows(piece, place):
        return lax.dynamic_slice(piece, (place, sensors, 0), (1, 2, NCOL))[0]

    wanted = [
        (p, at % 8)
        for own, down, last, up in ((0, 4, 7, 1), (5, 8, 3, 6))
        for p, at in ((own, z - 1), (own, z + 1), (down, last), (up, 0))
    ]
    spare = [spare_rows(pieces[p], at) for p, at in wanted + [(5, z)]]
    pieces, spare = lax.optimization_barrier((pieces, spare))
    spare = [v[0].astype(F32) + v[1].astype(F32) for v in spare]

    def pick(inside, wrapped, wraps, ends):
        return jnp.where(wraps, jnp.where(ends, 0.0, wrapped), inside)

    before = jnp.where(
        yh == 1,
        pick(spare[0], spare[2], z == 0, x == 0),
        pick(spare[4], spare[6], z == 0, x == 0),
    )
    after = jnp.where(
        yh == 0,
        pick(spare[1], spare[3], z == 7, x == 3),
        pick(spare[5], spare[7], z == 7, x == 3),
    )
    other = spare[8]
    coeff = jnp.concatenate(
        [
            before[-GY:],
            jnp.where(yh == 0, stiffness, other),
            jnp.where(yh == 0, other, stiffness),
            after[:GY],
        ]
    ).reshape(6, GY)

    spectra = pltpu.with_memory_space_constraint(spectra, pltpu.HBM)
    keep, give = adjoint(pieces, forward_table(gathered), inverse_table(steps_f), spectra)

    on = [(b, b + 1) for b in range(31)]
    outward = [(2 * d, 2 * b) for b, d in on] + [(2 * b + 1, 2 * d + 1) for b, d in on]
    inward = [(2 * b, 2 * d) for b, d in on] + [(2 * d + 1, 2 * b + 1) for b, d in on]

    field = [keep[p] + flip(give[p], "core").astype(F32) for p in range(4)]
    here = field[0] + flip(field[1].astype(BF), "yl").astype(F32)
    there = flip(field[2].astype(BF), "yh").astype(F32) + flip(
        field[3].astype(BF), "yh", "yl"
    ).astype(F32)
    here, there = here.reshape(2, GY, 8, NCOL), there.reshape(2, GY, 8, NCOL)
    first = lax.ppermute(here.astype(BF), ("x", "z", "yh"), outward).astype(F32)
    second = lax.ppermute(there.astype(BF), ("x", "z", "yh"), inward).astype(F32)
    grid = jnp.where(
        yh == 0,
        jnp.concatenate([second, here, there, first]),
        jnp.concatenate([first, there, here, second]),
    )
    for sweep in range(2):
        inner = grid[1:-1]
        sides = jnp.pad(inner, ((0, 0), (1, 1), (0, 0), (0, 0)))
        beside = grid[:-2] + grid[2:] + sides[:, :-2] + sides[:, 2:]
        rows = coeff if sweep == 0 else coeff[1:-1]
        grid = inner + rows[:, :, None, None] * (beside - 4.0 * inner)
    grid = grid.astype(BF).reshape(2, PTS, 8, NCOL)
    here = jnp.where(yh == 0, grid[0], grid[1])
    there = jnp.where(yh == 0, grid[1], grid[0])
    mine = [here, flip(here, "yl"), flip(there, "yh"), flip(there, "yh", "yl")]
    other = [flip(part, "core") for part in mine]

    outs = forward_map(mine, other, forward_table(steps_f), inverse_table(steps), spectra)
    near, back_across = outs[:5], outs[5:]

    def far_first(parts):
        low, high = from_x(parts[2], -1).astype(F32), from_x(parts[3], 1).astype(F32)
        up = jnp.concatenate([parts[1][:4] + low, parts[1][4:]]).astype(BF)
        down = jnp.concatenate([parts[4][:4], parts[4][4:] + high]).astype(BF)
        return up, down

    def gather_up(parts, up, down):
        return parts[0] + from_x(up, -1).astype(F32) + from_x(down, 1).astype(F32)

    across = gather_up(back_across, *far_first(back_across)).astype(BF)
    up, down = far_first(near)
    total = gather_up(near, up, down) + flip(across, "yh").astype(F32)
    total = lax.all_to_all(total.astype(BF), "z", 0, 0, tiled=True).astype(F32)
    return jnp.sum(total, axis=0, keepdims=True)[:, :sensors]


def solution(mesh):
    fine = Mesh(mesh.devices.reshape(4, 8, 2, 2, 2), ("x", "z", "yh", "yl", "core"))
    param, sensor = ("x", "z", "yh"), ("yl", "core")
    return jax.shard_map(
        shards,
        mesh=fine,
        in_specs=(P(param, sensor, None), P(None, None, sensor, param), P(param)),
        out_specs=P(param, sensor, None),
        check_vma=False,
    )
```
